256 devices in a mesh: pipe: 4 (over y), dp: 4 (over x), expert: 16 (over z, core).
Axes of the slice: x: 4, y: 4, z: 8, core: 2. Of those that a mesh axis runs over, the one named last changes fastest.
Arguments:
- block_input: bfloat16 [4, 8192, 3072], P('pipe', ('dp', 'expert')), may hold values from -6 to 6
- output_grad: bfloat16 [4, 8192, 3072], P('pipe', ('dp', 'expert')), may hold values from -6 to 6
- expert_ids: int32 [4, 8192, 6], P('pipe', ('dp', 'expert')), may hold values from 0 to 159, all different within a row
- gate_weights: float32 [4, 8192, 6], P('pipe', ('dp', 'expert')), may hold values from 0.25 to 2
- gate_proj: bfloat16 [4, 16, 3072, 1024], P('pipe', 'expert', None, 'dp'), may hold values from -0.109375 to 0.109375
- up_proj: bfloat16 [4, 16, 3072, 1024], P('pipe', 'expert', None, 'dp'), may hold values from -0.109375 to 0.109375
- down_proj: bfloat16 [4, 16, 1024, 3072], P('pipe', 'expert', 'dp'), may hold values from -0.1875 to 0.1875
Outputs:
- received_grad: bfloat16 [4, 8192, 3072], P('pipe', ('dp', 'expert'))
- gate_weight_grad: float32 [4, 8192, 6], P('pipe', ('dp', 'expert'))
- gate_proj_grad: bfloat16 [4, 16, 3072, 1024], P('pipe', 'expert', None, 'dp')
- up_proj_grad: bfloat16 [4, 16, 3072, 1024], P('pipe', 'expert', None, 'dp')
- down_proj_grad: bfloat16 [4, 16, 1024, 3072], P('pipe', 'expert', 'dp')
The draws below stay inside these ranges and needn't reach their ends.
Inputs may be any that keep to these rules, and one draw needn't show every extreme that they name: `expert_ids`: each token names 6 different experts.
All inputs are finite; a program needn't handle non-finite values.
Results may differ from the reference program's by a relative error of at most 0.006.
Values may be sent and summed in bfloat16 or wider, within the bound.
A program may use at most 128 MiB of HBM per device.

```python
import math
import jax
import jax.numpy as jnp
from jax import lax

D = 3072
H = 1024
ROUTED = 160
TOP = 6
TOK_DEV = 128
SECTIONS = 4
EXPERTS = 16
CAP = 8
TOKENS = 8192


def shard_levels(stream_key, extent, shards, low, largest):
    def one(dim, blocks):
        heights = jax.random.uniform(jax.random.fold_in(jax.random.fold_in(stream_key, 6), dim), (blocks,), jnp.float32, low / len(shards), largest / len(shards))
        return jnp.repeat(jnp.exp(heights), extent[dim] // blocks).reshape((-1,) + (1,) * (len(extent) - dim - 1))

    level = one(*shards[0])
    for cut in shards[1:]:
        level = level * one(*cut)
    return level


def picks_of(key, rows, amount, top, lift):
    sequence = jax.random.permutation(jax.random.fold_in(key, 1), amount)
    favour = sequence
    for power in range(3):
        favour = favour * favour // amount
    favour = favour * lift // amount
    tickets = jax.random.randint(jax.random.fold_in(key, 2), (rows, amount), 0, 4096) + favour
    sure = jax.random.permutation(jax.random.fold_in(key, 3), rows)[jnp.arange(amount) % rows]
    tickets = jnp.where(jnp.arange(rows)[:, None] == sure[None, :], 1 << 14, tickets)
    merit = tickets * amount + jnp.arange(amount)
    return lax.top_k(merit.astype(jnp.int32), top)[1].astype(jnp.int32)


def noise(stream_key, extent, deviation, limit, shards=(), kind=jnp.bfloat16):
    result = deviation * jax.random.normal(stream_key, extent, jnp.float32)
    if shards:
        result = result * shard_levels(stream_key, extent, shards, -0.22, 0.18)
    return jnp.clip(result, -limit, limit).astype(kind)


def setup_inputs(seed: int = 0) -> dict:
    key_list = jax.random.split(jax.random.key(seed), 8)
    return {
        "block_input": noise(key_list[0], (SECTIONS, TOKENS, D), 1.0, 6.0, ((0, 4), (1, 64))),
        "output_grad": noise(key_list[1], (SECTIONS, TOKENS, D), 1.0, 6.0, ((0, 4), (1, 64))),
        "expert_ids": picks_of(key_list[2], SECTIONS * TOKENS, ROUTED, TOP, 614).reshape((SECTIONS, TOKENS, TOP)),
        "gate_weights": jnp.clip(jnp.exp(math.log(2.0) - 2.0794415 * jax.random.uniform(key_list[3], (SECTIONS, TOKENS, TOP), jnp.float32) ** shard_levels(key_list[3], (SECTIONS, TOKENS, TOP), ((0, 4), (1, 64)), -0.2, 0.2)), 0.25, 2.0),
        "gate_proj": noise(key_list[4], (SECTIONS, EXPERTS, D, H), D ** -0.5, 0.109375, ((0, 4), (1, 16), (3, 4))),
        "up_proj": noise(key_list[5], (SECTIONS, EXPERTS, D, H), D ** -0.5, 0.109375, ((0, 4), (1, 16), (3, 4))),
        "down_proj": noise(key_list[6], (SECTIONS, EXPERTS, H, D), H ** -0.5, 0.1875, ((0, 4), (1, 16), (2, 4))),
    }


def section_backward(acts, grads, chosen_ids, weights, gate_w, up_w, down_w):
    blocks = TOKENS // TOK_DEV
    pairs = TOK_DEV * TOP
    block_ids = chosen_ids.reshape(blocks, pairs)
    columns = jnp.arange(EXPERTS, dtype=jnp.int32)
    onehot = (block_ids[:, :, None] == columns[None, None, :]).astype(jnp.int32)
    earlier = jnp.cumsum(onehot, axis=1) - onehot
    slot_rank = jnp.sum(earlier * onehot, axis=2)
    kept = (block_ids < EXPERTS) & (slot_rank < CAP)
    block_pos = jnp.arange(blocks, dtype=jnp.int32)[:, None]
    total = EXPERTS * blocks * CAP
    slot_index = jnp.where(kept, block_ids * (blocks * CAP) + block_pos * CAP + slot_rank, total).reshape(-1).astype(jnp.int32)
    pair_token = (jnp.arange(TOKENS * TOP, dtype=jnp.int32) // TOP).astype(jnp.int32)
    source_token = jnp.zeros((total + 1,), jnp.int32).at[slot_index].set(pair_token)[:total]
    slot_weight = jnp.zeros((total + 1,), weights.dtype).at[slot_index].set(weights.reshape(-1))[:total]
    filled = jnp.zeros((total + 1,), jnp.bool_).at[slot_index].set(True)[:total]
    disp_acts = jnp.where(filled[:, None], acts[source_token], jnp.zeros((), acts.dtype)).astype(acts.dtype)
    scaled = slot_weight[:, None] * grads[source_token].astype(jnp.float32)
    disp_grad = jnp.where(filled[:, None], scaled, jnp.zeros((), scaled.dtype)).astype(jnp.bfloat16)
    disp_acts = disp_acts.reshape(EXPERTS, blocks * CAP, D)
    disp_grad = disp_grad.reshape(EXPERTS, blocks * CAP, D)

    def expert_pass(items):
        rows_in, rows_grad, w_gate, w_upper, w_lower = items
        gate_pre = jnp.dot(rows_in, w_gate, preferred_element_type=jnp.float32)
        up_value = jnp.dot(rows_in, w_upper, preferred_element_type=jnp.float32)
        grad_hidden = jnp.dot(rows_grad, w_lower.T, preferred_element_type=jnp.float32)
        sigma_gate = jax.nn.sigmoid(gate_pre)
        swish = gate_pre * sigma_gate
        hidden = swish * up_value
        scores = jnp.sum(hidden * grad_hidden, axis=1)
        lower_grad = jnp.dot(hidden.astype(jnp.bfloat16).T, rows_grad, preferred_element_type=jnp.float32).astype(jnp.bfloat16)
        delta_gate = (grad_hidden * up_value * sigma_gate * (1.0 + gate_pre * (1.0 - sigma_gate))).astype(jnp.bfloat16)
        delta_up = (grad_hidden * swish).astype(jnp.bfloat16)
        gate_grad = jnp.dot(rows_in.T, delta_gate, preferred_element_type=jnp.float32).astype(jnp.bfloat16)
        upper_grad = jnp.dot(rows_in.T, delta_up, preferred_element_type=jnp.float32).astype(jnp.bfloat16)
        slot_grad = (jnp.dot(delta_gate, w_gate.T, preferred_element_type=jnp.float32)
                     + jnp.dot(delta_up, w_upper.T, preferred_element_type=jnp.float32)).astype(jnp.bfloat16)
        return gate_grad, upper_grad, lower_grad, slot_grad, scores

    results = lax.map(expert_pass, (disp_acts, disp_grad, gate_w, up_w, down_w))
    slot_grad = results[3].reshape(total, D).astype(jnp.float32)
    slot_grad = jnp.where(filled[:, None], slot_grad, jnp.zeros((), slot_grad.dtype))
    input_grad = jax.ops.segment_sum(slot_grad, source_token, num_segments=TOKENS).astype(jnp.bfloat16)
    scores = jnp.concatenate([results[4].reshape(total), jnp.zeros((1,), results[4].dtype)])
    weight_grad = (scores[slot_index] / weights.reshape(-1)).reshape(TOKENS, TOP)
    return input_grad, weight_grad, results[0], results[1], results[2]


def reference(block_input, output_grad, expert_ids, gate_weights, gate_proj, up_proj, down_proj):
    outputs = [section_backward(block_input[s], output_grad[s], expert_ids[s], gate_weights[s],
                              gate_proj[s], up_proj[s], down_proj[s]) for s in range(SECTIONS)]
    input_grads = jnp.stack([item[0] for item in outputs])
    received_grad = jnp.roll(input_grads, -1, axis=0)
    weight_grad = jnp.stack([item[1] for item in outputs])
    gate_grads = jnp.stack([item[2] for item in outputs])
    upper_grads = jnp.stack([item[3] for item in outputs])
    lower_grads = jnp.stack([item[4] for item in outputs])
    return (received_grad, weight_grad, gate_grads, upper_grads, lower_grads)
```

```python
import functools
import jax
import jax.numpy as jnp
from jax import lax
from jax.experimental import pallas as pl
from jax.experimental.pallas import tpu as pltpu
from jax.sharding import PartitionSpec as P

MESH = pl.DeviceIdType.MESH
CAP = 8
F32 = jnp.float32
BF16 = jnp.bfloat16
VMEM_LIMIT = 58 << 20
Z_ORDER = (0, 1, -1, 2, -2, 3, -3, 4)


def mod(value, count):
    return lax.rem(value + count, count)


def place():
    return lax.axis_index("pipe"), lax.axis_index("dp"), lax.axis_index("expert")


def remote(src, dst, send_sem, recv_sem, device):
    return pltpu.make_async_remote_copy(
        src_ref=src, dst_ref=dst, send_sem=send_sem, recv_sem=recv_sem,
        device_id=device, device_id_type=MESH)


def eight(row):
    return pl.ds(pl.multiple_of(row, 8), 8)


def slot_maps(ids_ref, slots, tokens):
    slot = lax.broadcasted_iota(jnp.int32, (slots, tokens), 0)
    expert = lax.shift_right_logical(slot, 3)
    rank = jnp.bitwise_and(slot, 7)
    return expert, rank


def fwd_kernel(nd, ne, x_ref, dy_ref, ids_ref, w_ref, rx, rg, sx, sg, smap_ref,
               xv, gv, lsem, zs, zr, xs, xr, fs, fr):
    p, i, e = place()
    z, c = e // 2, e % 2
    nz = ne // 2
    right, left = (p, mod(i + 1, nd), e), (p, mod(i - 1, nd), e)
    tokens, _ = x_ref.shape
    slots = ne * CAP
    chosen = ids_ref.shape[0]

    barrier = pltpu.get_barrier_semaphore()
    for d in range(1, ne):
        pl.semaphore_signal(barrier, inc=1, device_id=(p, i, lax.rem(e + d, ne)), device_id_type=MESH)
    for peer in (right, left):
        pl.semaphore_signal(barrier, inc=1, device_id=peer, device_id_type=MESH)

    expert, rank_of = slot_maps(ids_ref, slots, tokens)
    hit = jnp.zeros((slots, tokens), F32)
    weight = jnp.zeros((slots, tokens), F32)
    for k in range(chosen):
        same = ids_ref[k] == expert
        hit = jnp.where(same, 1.0, hit)
        weight = jnp.where(same, w_ref[k], weight)
    before = (lax.broadcasted_iota(jnp.int32, (tokens, tokens), 0)
              < lax.broadcasted_iota(jnp.int32, (tokens, tokens), 1))
    rank = jnp.dot(hit.astype(BF16), jnp.where(before, 1.0, 0.0).astype(BF16), preferred_element_type=F32)
    table = jnp.where(rank == rank_of.astype(F32), hit, 0.0)
    slot_weight = jnp.sum(table * weight, axis=1, keepdims=True)
    table = table.astype(BF16)
    smap_ref[...] = table
    xv[...] = jnp.dot(table, x_ref[...], preferred_element_type=F32).astype(BF16)
    gv[...] = (slot_weight * jnp.dot(table, dy_ref[...], preferred_element_type=F32)).astype(BF16)
    send, recv = (sx, sg), (rx, rg)
    stage = [pltpu.make_async_copy(xv, sx, lsem.at[0]), pltpu.make_async_copy(gv, sg, lsem.at[1])]
    for copy in stage:
        copy.start()
    for copy in stage:
        copy.wait()
    pl.semaphore_wait(barrier, ne - 1 + 2)

    def z_copy(kind, dz, dc):
        n = (dz % nz) * 2 + dc
        target = mod(z + dz, nz) * 2 + (c + dc - 2 * c * dc)
        return remote(send[kind].at[eight(target * CAP)], recv[kind].at[eight((i * ne + e) * CAP)],
                      zs.at[kind, n], zr.at[kind, n], (p, i, target))

    def own(kind):
        return pltpu.make_async_copy(send[kind].at[eight(e * CAP)], recv[kind].at[eight((i * ne + e) * CAP)],
                                     lsem.at[2 + kind])

    def group_rows(dp, g):
        chip = mod(z - Z_ORDER[g], nz)
        return pl.ds(pl.multiple_of((dp * ne + chip * 2) * CAP, 2 * CAP), 2 * CAP)

    def x_copy(kind, g, way):
        rows = group_rows(i, g)
        return remote(recv[kind].at[rows], recv[kind].at[rows], xs.at[kind, g, way], xr.at[kind, g, way],
                      (right, left)[way])

    def f_copy(kind, g):
        way = (g + kind) % 2
        rows = group_rows(mod(i - 1, nd) if way == 0 else mod(i + 1, nd), g)
        return remote(recv[kind].at[rows], recv[kind].at[rows], fs.at[kind, g], fr.at[kind, g], (right, left)[way])

    groups = len(Z_ORDER)

    def z_send(kind, g):
        for dc in (0, 1):
            if (Z_ORDER[g], dc) != (0, 0):
                z_copy(kind, Z_ORDER[g], dc).start()

    for kind in (0, 1):
        own(kind).start()
    for g in range(groups):
        z_send(0, g)
    steps = [(kind, g) for kind in (0, 1) for g in range(groups)]
    for t, (kind, g) in enumerate(steps):
        for dc in (0, 1):
            if (Z_ORDER[g], dc) == (0, 0):
                own(kind).wait()
            else:
                z_copy(kind, Z_ORDER[g], dc).wait_recv()
        for way in (0, 1):
            x_copy(kind, g, way).start()
        if kind == 0:
            z_send(1, g)
        if t:
            lk, lg = steps[t - 1]
            x_copy(lk, lg, (lg + lk) % 2).wait_recv()
            f_copy(lk, lg).start()
    lk, lg = steps[-1]
    x_copy(lk, lg, (lg + lk) % 2).wait_recv()
    f_copy(lk, lg).start()
    for kind, g in steps:
        x_copy(kind, g, 1 - (g + kind) % 2).wait_recv()
        f_copy(kind, g).wait_recv()
    for kind, g in steps:
        for dc in (0, 1):
            if (Z_ORDER[g], dc) != (0, 0):
                z_copy(kind, Z_ORDER[g], dc).wait_send()
        for way in (0, 1):
            x_copy(kind, g, way).wait_send()
        f_copy(kind, g).wait_send()


def dispatch(acts, grads, ids, weights, nd, ne):
    tokens, width = acts.shape
    rows = nd * ne * CAP
    slots = ne * CAP
    vmem, hbm = pl.BlockSpec(memory_space=pltpu.VMEM), pl.BlockSpec(memory_space=pltpu.HBM)
    dma = pltpu.SemaphoreType.DMA
    groups = len(Z_ORDER)
    wide = jax.ShapeDtypeStruct((rows, width), BF16)
    small = jax.ShapeDtypeStruct((slots, width), BF16)
    outs = pl.pallas_call(
        functools.partial(fwd_kernel, nd, ne),
        out_shape=(wide, wide, small, small, jax.ShapeDtypeStruct((slots, tokens), BF16)),
        in_specs=[vmem] * 4,
        out_specs=(hbm, hbm, hbm, hbm, vmem),
        scratch_shapes=[pltpu.VMEM((slots, width), BF16), pltpu.VMEM((slots, width), BF16),
                        dma((4,)), dma((2, ne)), dma((2, ne)), dma((2, groups, 2)), dma((2, groups, 2)),
                        dma((2, groups)), dma((2, groups))],
        compiler_params=pltpu.CompilerParams(collective_id=0, has_side_effects=True, vmem_limit_bytes=VMEM_LIMIT),
        name="dispatch",
    )(acts, grads, ids, weights)
    return outs[0], outs[1], outs[4]


def expert_kernel(rx_ref, rg_ref, wg_ref, wu_ref, wd_ref, part_ref, score_ref, dwg_ref, dwu_ref, dwd_ref,
                  delta, hid):
    rows, width = rx_ref.shape
    hs = wg_ref.shape[1]
    nt = (((1,), (1,)), ((), ()))
    tn = (((0,), (0,)), ((), ()))
    tall = 256

    def forward(k, _):
        r = pl.ds(pl.multiple_of(k * tall, tall), tall)
        xr, gr = rx_ref[r, :], rg_ref[r, :]
        gate = jnp.dot(xr, wg_ref[...], preferred_element_type=F32)
        up = jnp.dot(xr, wu_ref[...], preferred_element_type=F32)
        gh = lax.dot_general(gr, wd_ref[...], nt, preferred_element_type=F32)
        sig = jax.nn.sigmoid(gate)
        swish = gate * sig
        hidden = swish * up
        score = jnp.sum(hidden * gh, axis=1, keepdims=True)
        lane = lax.broadcasted_iota(jnp.int32, (tall, 128), 1)
        row = jnp.bitwise_and(lax.broadcasted_iota(jnp.int32, (tall, 128), 0), CAP - 1)
        spread = jnp.where(lane == row, jnp.broadcast_to(score, (tall, 128)), 0.0)
        blocks = tall // CAP
        score_ref[pl.ds(k * blocks, blocks)] = jnp.sum(spread.reshape(blocks, CAP, 128), axis=1, keepdims=True)
        hid[r, :] = hidden.astype(BF16)
        delta[r, 0:hs] = (gh * up * sig * (1.0 + gate * (1.0 - sig))).astype(BF16)
        delta[r, hs:] = (gh * swish).astype(BF16)
        return 0

    lax.fori_loop(0, rows // tall, forward, 0)
    wide = 256
    dl, hd = delta[...], hid[...]

    def backward(t, _):
        cols = pl.ds(pl.multiple_of(t * wide, wide), wide)
        part = lax.dot_general(dl[:, :hs], wg_ref[cols, :], nt, preferred_element_type=F32)
        part += lax.dot_general(dl[:, hs:], wu_ref[cols, :], nt, preferred_element_type=F32)
        part_ref[:, cols] = part.astype(BF16)
        both = lax.dot_general(rx_ref[:, cols], dl, tn, preferred_element_type=F32).astype(BF16)
        dwg_ref[cols, :] = both[:, :hs]
        dwu_ref[cols, :] = both[:, hs:]
        dwd_ref[:, cols] = lax.dot_general(hd, rg_ref[:, cols], tn, preferred_element_type=F32).astype(BF16)
        return 0

    lax.fori_loop(0, width // wide, backward, 0)


def experts(rx, rg, wg, wu, wd):
    rows, width = rx.shape
    hs = wg.shape[1]
    vmem = pl.BlockSpec(memory_space=pltpu.VMEM)
    return pl.pallas_call(
        expert_kernel,
        out_shape=(jax.ShapeDtypeStruct((rows, width), BF16), jax.ShapeDtypeStruct((rows // CAP, 1, 128), F32),
                   jax.ShapeDtypeStruct((width, hs), BF16), jax.ShapeDtypeStruct((width, hs), BF16),
                   jax.ShapeDtypeStruct((hs, width), BF16)),
        in_specs=[vmem] * 5,
        out_specs=(vmem,) * 5,
        scratch_shapes=[pltpu.VMEM((rows, 2 * hs), BF16), pltpu.VMEM((rows, hs), BF16)],
        compiler_params=pltpu.CompilerParams(vmem_limit_bytes=VMEM_LIMIT),
        name="experts",
    )(rx, rg, wg, wu, wd)


def ret_kernel(nd, ne, pieces, part, score, smap, ids_ref, w_ref, out_ref, gwg_ref, rows_hbm, fin_hbm,
               b1, b2, bu, fin, back, snext, sc3, own_score, slot_score,
               lsem, s1s, s1r, s2s, s2r, sus, sur, zs, zr, cs, cr, es, er, ms, mr):
    p, i, e = place()
    npipe = lax.axis_size("pipe")
    slots, tokens = smap.shape
    width = part.shape[1]
    right, left = (p, mod(i + 1, nd), e), (p, mod(i - 1, nd), e)
    prev, nxt = mod(p - 1, npipe), mod(p + 1, npipe)
    chosen = ids_ref.shape[0]

    barrier = pltpu.get_barrier_semaphore()

    def greet(device):
        pl.semaphore_signal(barrier, inc=1, device_id=device, device_id_type=MESH)

    for d in range(1, nd):
        greet((p, mod(i + d, nd), e))
    for d in range(1, ne):
        greet((p, i, lax.rem(e + d, ne)))
    for d in range(ne):
        greet((prev, i, lax.rem(e + d, ne)))
        greet((nxt, i, lax.rem(e + d, ne)))
    pl.semaphore_wait(barrier, nd - 1 + ne - 1 + 2 * ne)

    def chunk(dp):
        return pl.ds(pl.multiple_of(dp * slots, slots), slots)

    def one(dp):
        return mod(i + dp, nd)

    cols = [pl.ds(start, size) for start, size in pieces]
    sides = (right, left)

    def step1(q):
        return remote(part.at[chunk(one(2)), cols[q]], b1.at[:, cols[q]], s1s.at[q], s1r.at[q], sides[q % 2])

    def plain(q):
        src = one(-1) if q % 2 == 0 else one(1)
        return remote(part.at[chunk(src), cols[q]], bu.at[:, cols[q]], sus.at[q], sur.at[q], sides[1 - q % 2])

    def step2(q):
        return remote(b1.at[:, cols[q]], b2.at[:, cols[q]], s2s.at[q], s2r.at[q], sides[q % 2])

    def map_copy():
        return remote(smap, snext, ms.at[0], mr.at[0], (prev, i, e))

    def score_x(d):
        return remote(score.at[pl.ds(one(d) * ne, ne)], sc3.at[d - 1], cs.at[d - 1], cr.at[d - 1], (p, one(d), e))

    def score_z(d):
        target = lax.rem(e + d, ne)
        return remote(own_score.at[target], slot_score.at[e], es.at[d], er.at[d], (p, i, target))

    pairs = len(pieces) // 2
    pair_cols = [pl.ds(pieces[2 * q][0], pieces[2 * q][1] + pieces[2 * q + 1][1]) for q in range(pairs)]

    def z_copy(pair, d):
        target = lax.rem(e + d, ne)
        return remote(fin_hbm.at[eight(target * CAP), pair_cols[pair]], rows_hbm.at[eight(e * CAP), pair_cols[pair]],
                      zs.at[pair, d], zr.at[pair, d], (prev, i, target))

    for q in range(len(pieces)):
        step1(q).start()
        if q % 2:
            plain(q - 1).start()
            plain(q).start()
        if q == 1:
            map_copy().start()
            for d in range(1, nd):
                score_x(d).start()

    def finish(pair):
        for q in (2 * pair, 2 * pair + 1):
            plain(q).wait_recv()
            step2(q).wait_recv()
        here = pair_cols[pair]
        total = part[chunk(i), here].astype(F32) + b2[:, here].astype(F32) + bu[:, here].astype(F32)
        fin[:, here] = total.astype(BF16)
        copy = pltpu.make_async_copy(fin.at[:, here], fin_hbm.at[:, here], lsem.at[0])
        copy.start()
        copy.wait()
        for d in range(ne):
            z_copy(pair, d).start()

    for pair in range(pairs):
        for q in (2 * pair, 2 * pair + 1):
            step1(q).wait_recv()
            mine = one(1) if q % 2 == 0 else one(-1)
            total = part[chunk(mine), cols[q]].astype(F32) + b1[:, cols[q]].astype(F32)
            b1[:, cols[q]] = total.astype(BF16)
            step2(q).start()
        if pair:
            finish(pair - 1)
        else:
            for d in range(1, nd):
                score_x(d).wait_recv()
            own_score[...] = score[pl.ds(i * ne, ne)] + sc3[0] + sc3[1] + sc3[2]
            slot_score[e] = own_score[e]
            for d in range(1, ne):
                score_z(d).start()
    finish(pairs - 1)

    for d in range(1, ne):
        score_z(d).wait_recv()
    column = jnp.broadcast_to(slot_score[...], (ne, CAP, 128)).reshape(slots, 128)
    expert, rank = slot_maps(ids_ref, slots, tokens)
    lane = lax.broadcasted_iota(jnp.int32, (slots, 128), 1)
    column = jnp.sum(jnp.where(lane == jnp.bitwise_and(lax.broadcasted_iota(jnp.int32, (slots, 128), 0), CAP - 1),
                               column, 0.0), axis=1, keepdims=True)
    spread = smap[...].astype(F32) * column
    for k in range(chosen):
        picked = jnp.sum(jnp.where(ids_ref[k] == expert, spread, 0.0), axis=0, keepdims=True)
        gwg_ref[k] = picked / w_ref[k]
    map_copy().wait_recv()
    tn = (((0,), (0,)), ((), ()))
    for pair in range(pairs):
        for d in range(ne):
            z_copy(pair, d).wait_recv()
        here = pair_cols[pair]
        copy = pltpu.make_async_copy(rows_hbm.at[:, here], back.at[:, here], lsem.at[1])
        copy.start()
        copy.wait()
        out_ref[:, here] = lax.dot_general(snext[...], back[:, here], tn, preferred_element_type=F32).astype(BF16)
    for q in range(len(pieces)):
        step1(q).wait_send()
        plain(q).wait_send()
        step2(q).wait_send()
    map_copy().wait_send()
    for d in range(1, nd):
        score_x(d).wait_send()
    for d in range(1, ne):
        score_z(d).wait_send()
    for pair in range(pairs):
        for d in range(ne):
            z_copy(pair, d).wait_send()


def combine(part, score, smap, ids, weights, nd, ne):
    slots, tokens = smap.shape
    width = part.shape[1]
    pieces = [(start, 512) for start in range(0, width, 512)]
    vmem, hbm = pl.BlockSpec(memory_space=pltpu.VMEM), pl.BlockSpec(memory_space=pltpu.HBM)
    dma = pltpu.SemaphoreType.DMA
    block = pltpu.VMEM((slots, width), BF16)
    small = jax.ShapeDtypeStruct((slots, width), BF16)
    n = len(pieces)
    outs = pl.pallas_call(
        functools.partial(ret_kernel, nd, ne, pieces),
        out_shape=(jax.ShapeDtypeStruct((tokens, width), BF16), jax.ShapeDtypeStruct(ids.shape, F32), small, small),
        in_specs=[vmem] * 5,
        out_specs=(vmem, vmem, hbm, hbm),
        scratch_shapes=[block] * 5 + [
            pltpu.VMEM((slots, tokens), BF16), pltpu.VMEM((nd - 1, ne, 1, 128), F32), pltpu.VMEM((ne, 1, 128), F32),
            pltpu.VMEM((ne, 1, 128), F32), dma((2,))] + [dma((n,))] * 6 + [dma((n // 2, ne))] * 2
            + [dma((nd - 1,))] * 2 + [dma((ne,))] * 2 + [dma((1,))] * 2,
        compiler_params=pltpu.CompilerParams(collective_id=1, has_side_effects=True, vmem_limit_bytes=VMEM_LIMIT),
        name="combine",
    )(part, score, smap, ids, weights)
    return outs[0], outs[1]


def shards(block_input, output_grad, expert_ids, gate_weights, gate_proj, up_proj, down_proj):
    nd, ne = lax.axis_size("dp"), lax.axis_size("expert")
    ids = jnp.transpose(expert_ids, (2, 0, 1))
    weights = jnp.transpose(gate_weights, (2, 0, 1))
    rx, rg, smap = dispatch(block_input[0], output_grad[0], ids, weights, nd, ne)
    part, score, dwg, dwu, dwd = experts(rx, rg, gate_proj[0, 0], up_proj[0, 0], down_proj[0, 0])
    received, gwg = combine(part, score, smap, ids, weights, nd, ne)
    return (received[None], jnp.transpose(gwg, (1, 2, 0)), dwg[None, None], dwu[None, None], dwd[None, None])


def solution(mesh):
    in_specs = (
        P("pipe", ("dp", "expert"), None),
        P("pipe", ("dp", "expert"), None),
        P("pipe", ("dp", "expert"), None),
        P("pipe", ("dp", "expert"), None),
        P("pipe", "expert", None, "dp"),
        P("pipe", "expert", None, "dp"),
        P("pipe", "expert", "dp", None),
    )
    out_specs = (
        P("pipe", ("dp", "expert"), None),
        P("pipe", ("dp", "expert"), None),
        P("pipe", "expert", None, "dp"),
        P("pipe", "expert", None, "dp"),
        P("pipe", "expert", "dp", None),
    )
    return jax.shard_map(shards, mesh=mesh, in_specs=in_specs, out_specs=out_specs, check_vma=False)
```

```python
import functools
import jax
import jax.numpy as jnp
from jax import lax
from jax.experimental import pallas as pl
from jax.experimental.pallas import tpu as pltpu
from jax.sharding import PartitionSpec as P

MESH = pl.DeviceIdType.MESH
CAP = 8
F32 = jnp.float32
BF16 = jnp.bfloat16
VMEM_LIMIT = 58 << 20
Z_ORDER = (0, 1, -1, 2, -2, 3, -3, 4)


def mod(value, count):
    return lax.rem(value + count, count)


def place():
    return lax.axis_index("pipe"), lax.axis_index("dp"), lax.axis_index("expert")


def remote(src, dst, send_sem, recv_sem, device):
    return pltpu.make_async_remote_copy(
        src_ref=src, dst_ref=dst, send_sem=send_sem, recv_sem=recv_sem,
        device_id=device, device_id_type=MESH)


def eight(row):
    return pl.ds(pl.multiple_of(row, 8), 8)


def slot_maps(ids_ref, slots, tokens):
    slot = lax.broadcasted_iota(jnp.int32, (slots, tokens), 0)
    expert = lax.shift_right_logical(slot, 3)
    rank = jnp.bitwise_and(slot, 7)
    return expert, rank


def routed_kernel(nd, ne, pieces, x_ref, dy_ref, ids_ref, w_ref, wg_hbm, wu_hbm, wd_hbm,
                  rows_hbm, next_hbm, score_hbm, smap_ref, rx_hbm, rg_hbm, delta_hbm, hidden_hbm,
                  sx, sg, rx, rg, wg, wu, wd, gu, delta, hid, part, b1, b2, bu, fin, score, sc3, own_score,
                  lsem, zs, zr, xs, xr, fs, fr, s1s, s1r, s2s, s2r, sus, sur, ys, yr, cs, cr, es, er, ms, mr):
    p, i, e = place()
    z, c = e // 2, e % 2
    nz = ne // 2
    npipe = lax.axis_size("pipe")
    tokens, width = x_ref.shape
    slots = ne * CAP
    chosen = ids_ref.shape[0]
    hs = wg.shape[1]
    groups = len(Z_ORDER)
    nt = (((1,), (1,)), ((), ()))
    right, left = (p, mod(i + 1, nd), e), (p, mod(i - 1, nd), e)
    sides = (right, left)
    prev, nxt = mod(p - 1, npipe), mod(p + 1, npipe)

    barrier = pltpu.get_barrier_semaphore()

    def greet(device):
        pl.semaphore_signal(barrier, inc=1, device_id=device, device_id_type=MESH)

    for d in range(1, nd):
        greet((p, mod(i + d, nd), e))
    for d in range(1, ne):
        greet((p, i, lax.rem(e + d, ne)))
    for d in range(ne):
        greet((prev, i, lax.rem(e + d, ne)))
        greet((nxt, i, lax.rem(e + d, ne)))

    loads = [pltpu.make_async_copy(a, b, lsem.at[n]) for n, (a, b) in enumerate(
        ((wg_hbm, wg), (wu_hbm, wu), (wd_hbm, wd)))]
    for copy in loads:
        copy.start()

    expert, rank_of = slot_maps(ids_ref, slots, tokens)
    hit = jnp.zeros((slots, tokens), F32)
    weight = jnp.zeros((slots, tokens), F32)
    for k in range(chosen):
        same = ids_ref[k] == expert
        hit = jnp.where(same, 1.0, hit)
        weight = jnp.where(same, w_ref[k], weight)
    before = (lax.broadcasted_iota(jnp.int32, (tokens, tokens), 0)
              < lax.broadcasted_iota(jnp.int32, (tokens, tokens), 1))
    rank = jnp.dot(hit.astype(BF16), jnp.where(before, 1.0, 0.0).astype(BF16), preferred_element_type=F32)
    table = jnp.where(rank == rank_of.astype(F32), hit, 0.0)
    slot_weight = jnp.sum(table * weight, axis=1, keepdims=True)
    table = table.astype(BF16)
    smap_ref[...] = table
    sx[...] = jnp.dot(table, x_ref[...], preferred_element_type=F32).astype(BF16)
    pl.semaphore_wait(barrier, nd - 1 + ne - 1 + 2 * ne)

    send, recv = (sx, sg), (rx, rg)

    def z_copy(kind, dz, dc):
        n = (dz % nz) * 2 + dc
        target = mod(z + dz, nz) * 2 + (c + dc - 2 * c * dc)
        return remote(send[kind].at[eight(target * CAP)], recv[kind].at[eight((i * ne + e) * CAP)],
                      zs.at[kind, n], zr.at[kind, n], (p, i, target))

    def own(kind):
        return pltpu.make_async_copy(send[kind].at[eight(e * CAP)], recv[kind].at[eight((i * ne + e) * CAP)],
                                     lsem.at[3 + kind])

    def group_rows(dp, g):
        chip = mod(z - Z_ORDER[g], nz)
        return pl.ds(pl.multiple_of((dp * ne + chip * 2) * CAP, 2 * CAP), 2 * CAP)

    def x_copy(kind, g, way):
        rows = group_rows(i, g)
        return remote(recv[kind].at[rows], recv[kind].at[rows], xs.at[kind, g, way], xr.at[kind, g, way], sides[way])

    def f_way(kind, g):
        return (g + kind) % 2

    def f_copy(kind, g):
        way = f_way(kind, g)
        rows = group_rows(mod(i - 1, nd) if way == 0 else mod(i + 1, nd), g)
        return remote(recv[kind].at[rows], recv[kind].at[rows], fs.at[kind, g], fr.at[kind, g], sides[way])

    def z_send(kind, g):
        for dc in (0, 1):
            if (Z_ORDER[g], dc) != (0, 0):
                z_copy(kind, Z_ORDER[g], dc).start()

    def z_step(kind, g):
        for dc in (0, 1):
            if (Z_ORDER[g], dc) == (0, 0):
                own(kind).wait()
            else:
                z_copy(kind, Z_ORDER[g], dc).wait_recv()
        for way in (0, 1):
            x_copy(kind, g, way).start()

    def forward(kind, g):
        x_copy(kind, g, f_way(kind, g)).wait_recv()
        f_copy(kind, g).start()

    def map_copy():
        return remote(smap_ref, next_hbm, ms.at[0], mr.at[0], (prev, i, e))

    own(0).start()
    for g in range(groups):
        z_send(0, g)
    sg[...] = (slot_weight * jnp.dot(table, dy_ref[...], preferred_element_type=F32)).astype(BF16)
    own(1).start()
    map_copy().start()

    def one(dp):
        return mod(i + dp, nd)

    def chunk(dp):
        return pl.ds(pl.multiple_of(dp * slots, slots), slots)

    def inner(dp):
        r = chunk(one(dp))
        gu[r, 0:hs] = jnp.dot(rx[r, :], wg[...], preferred_element_type=F32)
        gu[r, hs:] = jnp.dot(rx[r, :], wu[...], preferred_element_type=F32)

    def act(dp):
        r = chunk(one(dp))
        gate, up = gu[r, 0:hs], gu[r, hs:]
        gh = lax.dot_general(rg[r, :], wd[...], nt, preferred_element_type=F32)
        sig = jax.nn.sigmoid(gate)
        swish = gate * sig
        hidden = swish * up
        total = jnp.sum(hidden * gh, axis=1, keepdims=True)
        lane = lax.broadcasted_iota(jnp.int32, (slots, 128), 1)
        row = jnp.bitwise_and(lax.broadcasted_iota(jnp.int32, (slots, 128), 0), CAP - 1)
        spread = jnp.where(lane == row, jnp.broadcast_to(total, (slots, 128)), 0.0)
        score[pl.ds(one(dp) * ne, ne)] = jnp.sum(spread.reshape(ne, CAP, 128), axis=1, keepdims=True)
        hid[r, :] = hidden.astype(BF16)
        delta[r, 0:hs] = (gh * up * sig * (1.0 + gate * (1.0 - sig))).astype(BF16)
        delta[r, hs:] = (gh * swish).astype(BF16)

    def partial(dp):
        r = chunk(one(dp))
        dg, du = delta[r, 0:hs], delta[r, hs:]
        wide = 512
        for t in range(width // wide):
            cut = slice(t * wide, (t + 1) * wide)
            value = lax.dot_general(dg, wg[cut, :], nt, preferred_element_type=F32)
            value += lax.dot_general(du, wu[cut, :], nt, preferred_element_type=F32)
            part[r, cut] = value.astype(BF16)

    for g in range(groups):
        z_step(0, g)
        z_send(1, g)
        if g:
            forward(0, g - 1)
    for copy in loads:
        copy.wait()
    order = (0, -1, 1, 2)
    for g in range(groups):
        z_step(1, g)
        forward(*((1, g - 1) if g else (0, groups - 1)))
        if 3 <= g < 7:
            if g == 4:
                for h in range(groups):
                    x_copy(0, h, 1 - f_way(0, h)).wait_recv()
            if g == 6:
                for h in range(groups):
                    f_copy(0, h).wait_recv()
            inner(order[g - 3])
    act(0)
    forward(1, groups - 1)
    for g in range(groups):
        x_copy(1, g, 1 - f_way(1, g)).wait_recv()

    cols = [pl.ds(start, size) for start, size in pieces]

    def step1(q):
        return remote(part.at[chunk(one(2)), cols[q]], b1.at[:, cols[q]], s1s.at[q], s1r.at[q], sides[q % 2])

    def plain(q):
        src = one(-1) if q % 2 == 0 else one(1)
        return remote(part.at[chunk(src), cols[q]], bu.at[:, cols[q]], sus.at[q], sur.at[q], sides[1 - q % 2])

    def step2(q):
        return remote(b1.at[:, cols[q]], b2.at[:, cols[q]], s2s.at[q], s2r.at[q], sides[q % 2])

    def score_x(d):
        return remote(score.at[pl.ds(one(d) * ne, ne)], sc3.at[d - 1], cs.at[d - 1], cr.at[d - 1], (p, one(d), e))

    def score_z(d):
        target = lax.rem(e + d, ne)
        return remote(own_score.at[target], score_hbm.at[e], es.at[d], er.at[d], (p, i, target))

    def score_own():
        return pltpu.make_async_copy(own_score.at[e], score_hbm.at[e], lsem.at[5])

    pairs = len(pieces) // 2
    pair_cols = [pl.ds(pieces[2 * q][0], pieces[2 * q][1] + pieces[2 * q + 1][1]) for q in range(pairs)]

    def y_copy(pair, d):
        target = lax.rem(e + d, ne)
        return remote(fin.at[eight(target * CAP), pair_cols[pair]], rows_hbm.at[eight(e * CAP), pair_cols[pair]],
                      ys.at[pair, d], yr.at[pair, d], (prev, i, target))

    def both(copy, pair):
        for q in (2 * pair, 2 * pair + 1):
            copy(q).start()

    def middle(pair):
        for q in (2 * pair, 2 * pair + 1):
            step1(q).wait_recv()
            mine = one(1) if q % 2 == 0 else one(-1)
            total = part[chunk(mine), cols[q]].astype(F32) + b1[:, cols[q]].astype(F32)
            b1[:, cols[q]] = total.astype(BF16)
            step2(q).start()

    def finish(pair):
        for q in (2 * pair, 2 * pair + 1):
            plain(q).wait_recv()
            step2(q).wait_recv()
        here = pair_cols[pair]
        total = part[chunk(i), here].astype(F32) + b2[:, here].astype(F32) + bu[:, here].astype(F32)
        fin[:, here] = total.astype(BF16)
        for d in range(ne):
            y_copy(pair, d).start()

    act(-1)
    act(1)
    partial(-1)
    partial(1)
    both(plain, 0)
    both(plain, 1)
    for g in range(groups):
        f_copy(1, g).wait_recv()
    act(2)
    partial(2)
    both(step1, 0)
    both(step1, 1)
    for d in range(1, nd):
        score_x(d).start()
    saves = [pltpu.make_async_copy(a, b, lsem.at[6 + n]) for n, (a, b) in enumerate(
        ((rx, rx_hbm), (rg, rg_hbm), (delta, delta_hbm), (hid, hidden_hbm)))]
    for copy in saves:
        copy.start()
    partial(0)
    middle(0)
    both(plain, 2)
    both(step1, 2)
    middle(1)
    finish(0)
    for d in range(1, nd):
        score_x(d).wait_recv()
    own_score[...] = score[pl.ds(i * ne, ne)] + sc3[0] + sc3[1] + sc3[2]
    score_own().start()
    for d in range(1, ne):
        score_z(d).start()
    middle(2)
    finish(1)
    finish(2)

    for copy in saves:
        copy.wait()
    for kind in (0, 1):
        for g in range(groups):
            for dc in (0, 1):
                if (Z_ORDER[g], dc) != (0, 0):
                    z_copy(kind, Z_ORDER[g], dc).wait_send()
            for way in (0, 1):
                x_copy(kind, g, way).wait_send()
            f_copy(kind, g).wait_send()
    for q in range(len(pieces)):
        step1(q).wait_send()
        plain(q).wait_send()
        step2(q).wait_send()
    map_copy().wait_send()
    map_copy().wait_recv()
    score_own().wait()
    for d in range(1, nd):
        score_x(d).wait_send()
    for d in range(1, ne):
        score_z(d).wait_send()
        score_z(d).wait_recv()
    for pair in range(pairs):
        for d in range(ne):
            y_copy(pair, d).wait_send()
            y_copy(pair, d).wait_recv()


def routed(acts, grads, ids, weights, wg, wu, wd, nd, ne):
    tokens, width = acts.shape
    hs = wg.shape[1]
    slots = ne * CAP
    rows = nd * slots
    edges = ((0, 640), (1280, 512), (2304, 384))
    pieces = [(start + half * size, size) for start, size in edges for half in (0, 1)]
    vmem, hbm = pl.BlockSpec(memory_space=pltpu.VMEM), pl.BlockSpec(memory_space=pltpu.HBM)
    dma = pltpu.SemaphoreType.DMA
    groups, n = len(Z_ORDER), len(pieces)
    shape = jax.ShapeDtypeStruct
    block = pltpu.VMEM((slots, width), BF16)
    full = pltpu.VMEM((rows, width), BF16)
    return pl.pallas_call(
        functools.partial(routed_kernel, nd, ne, pieces),
        out_shape=(shape((slots, width), BF16), shape((slots, tokens), BF16), shape((ne, 1, 128), F32),
                   shape((slots, tokens), BF16), shape((rows, width), BF16), shape((rows, width), BF16),
                   shape((rows, 2 * hs), BF16), shape((rows, hs), BF16)),
        in_specs=[vmem] * 4 + [hbm] * 3,
        out_specs=(hbm, hbm, hbm, vmem, hbm, hbm, hbm, hbm),
        scratch_shapes=[block, block, full, full, pltpu.VMEM(wg.shape, BF16), pltpu.VMEM(wu.shape, BF16),
                        pltpu.VMEM(wd.shape, BF16), pltpu.VMEM((rows, 2 * hs), F32), pltpu.VMEM((rows, 2 * hs), BF16),
                        pltpu.VMEM((rows, hs), BF16), full, block, block, block, block,
                        pltpu.VMEM((nd * ne, 1, 128), F32), pltpu.VMEM((nd - 1, ne, 1, 128), F32),
                        pltpu.VMEM((ne, 1, 128), F32),
                        dma((10,)), dma((2, ne)), dma((2, ne)), dma((2, groups, 2)), dma((2, groups, 2)),
                        dma((2, groups)), dma((2, groups))] + [dma((n,))] * 6 + [dma((n // 2, ne))] * 2
        + [dma((nd - 1,))] * 2 + [dma((ne,))] * 2 + [dma((1,))] * 2,
        compiler_params=pltpu.CompilerParams(collective_id=0, has_side_effects=True, vmem_limit_bytes=VMEM_LIMIT),
        name="routed",
    )(acts, grads, ids, weights, wg, wu, wd)


def local_kernel(rx, rg, delta, hid, rows, snext, smap, score, ids_ref, w_ref, out, gwg, dwg, dwu, dwd):
    tn = (((0,), (0,)), ((), ()))
    hs = hid.shape[1]
    slots, tokens = smap.shape

    @pl.when(pl.program_id(0) == 0)
    def _():
        ne = slots // CAP
        column = jnp.broadcast_to(score[...], (ne, CAP, 128)).reshape(slots, 128)
        expert, _ = slot_maps(ids_ref, slots, tokens)
        lane = lax.broadcasted_iota(jnp.int32, (slots, 128), 1)
        row = jnp.bitwise_and(lax.broadcasted_iota(jnp.int32, (slots, 128), 0), CAP - 1)
        column = jnp.sum(jnp.where(lane == row, column, 0.0), axis=1, keepdims=True)
        spread = smap[...].astype(F32) * column
        for k in range(ids_ref.shape[0]):
            picked = jnp.sum(jnp.where(ids_ref[k] == expert, spread, 0.0), axis=0, keepdims=True)
            gwg[k] = picked / w_ref[k]

    out[...] = lax.dot_general(snext[...], rows[...], tn, preferred_element_type=F32).astype(BF16)
    both = lax.dot_general(rx[...], delta[...], tn, preferred_element_type=F32).astype(BF16)
    dwg[...] = both[:, :hs]
    dwu[...] = both[:, hs:]
    dwd[...] = lax.dot_general(hid[...], rg[...], tn, preferred_element_type=F32).astype(BF16)


def local(rows, snext, score, smap, rx, rg, delta, hid, ids, weights):
    count, width = rx.shape
    hs = hid.shape[1]
    slots, tokens = smap.shape
    wide = 512

    def whole(array):
        return pl.BlockSpec(array.shape, lambda t: (0,) * array.ndim)

    def across(height):
        return pl.BlockSpec((height, wide), lambda t: (0, t))

    down = pl.BlockSpec((wide, hs), lambda t: (t, 0))
    shape = jax.ShapeDtypeStruct
    return pl.pallas_call(
        local_kernel,
        grid=(width // wide,),
        out_shape=(shape((tokens, width), BF16), shape(ids.shape, F32), shape((width, hs), BF16),
                   shape((width, hs), BF16), shape((hs, width), BF16)),
        in_specs=[across(count), across(count), whole(delta), whole(hid), across(slots), whole(snext), whole(smap),
                  whole(score), whole(ids), whole(weights)],
        out_specs=(across(tokens), whole(ids), down, down, across(hs)),
        compiler_params=pltpu.CompilerParams(vmem_limit_bytes=VMEM_LIMIT),
        name="local",
    )(rx, rg, delta, hid, rows, snext, smap, score, ids, weights)


def shards(block_input, output_grad, expert_ids, gate_weights, gate_proj, up_proj, down_proj):
    nd, ne = lax.axis_size("dp"), lax.axis_size("expert")
    ids = jnp.transpose(expert_ids, (2, 0, 1))
    weights = jnp.transpose(gate_weights, (2, 0, 1))
    outs = routed(block_input[0], output_grad[0], ids, weights, gate_proj[0, 0], up_proj[0, 0], down_proj[0, 0],
                  nd, ne)
    received, gwg, dwg, dwu, dwd = local(*outs, ids, weights)
    return (received[None], jnp.transpose(gwg, (1, 2, 0)), dwg[None, None], dwu[None, None], dwd[None, None])


def solution(mesh):
    in_specs = (
        P("pipe", ("dp", "expert"), None),
        P("pipe", ("dp", "expert"), None),
        P("pipe", ("dp", "expert"), None),
        P("pipe", ("dp", "expert"), None),
        P("pipe", "expert", None, "dp"),
        P("pipe", "expert", None, "dp"),
        P("pipe", "expert", "dp", None),
    )
    out_specs = (
        P("pipe", ("dp", "expert"), None),
        P("pipe", ("dp", "expert"), None),
        P("pipe", "expert", None, "dp"),
        P("pipe", "expert", None, "dp"),
        P("pipe", "expert", "dp", None),
    )
    return jax.shard_map(shards, mesh=mesh, in_specs=in_specs, out_specs=out_specs, check_vma=False)
```

```python
import functools
import jax
import jax.numpy as jnp
from jax import lax
from jax.experimental import pallas as pl
from jax.experimental.pallas import tpu as pltpu
from jax.sharding import PartitionSpec as P

MESH = pl.DeviceIdType.MESH
CAP = 8
F32 = jnp.float32
BF16 = jnp.bfloat16
VMEM_LIMIT = 58 << 20
Z_PLACES = (0, 1, -1, 2, -2, 3, -3, 4)
LOOK = 2
LAG = 4
PAIRS = ((1536, 1536), (1280, 1024, 768))


def mod(value, count):
    return lax.rem(value + count, count)


def place():
    return lax.axis_index("pipe"), lax.axis_index("dp"), lax.axis_index("expert")


def remote(src, dst, send_sem, recv_sem, device):
    return pltpu.make_async_remote_copy(
        src_ref=src, dst_ref=dst, send_sem=send_sem, recv_sem=recv_sem,
        device_id=device, device_id_type=MESH)


def eight(row):
    return pl.ds(pl.multiple_of(row, 8), 8)


def slot_maps(ids_ref, slots, tokens):
    slot = lax.broadcasted_iota(jnp.int32, (slots, tokens), 0)
    expert = lax.shift_right_logical(slot, 3)
    rank = jnp.bitwise_and(slot, 7)
    return expert, rank


def routed_kernel(nd, ne, pieces, x_hbm, dy_hbm, ids_hbm, w_hbm, wg_hbm, wu_hbm, wd_hbm,
                  rows_hbm, next_hbm, score_hbm, smap_hbm, rx_hbm, rg_hbm, delta_hbm, hidden_hbm,
                  xv, dyv, ids, wts, smap, sx, sg, rx, rg, wg, wu, wd, gu, delta, hid, part, b1, b2, bu, fin,
                  score, sc3, own_score, lsem, zs, zr, xs, xr, fs, fr, s1s, s1r, s2s, s2r, sus, sur, ys, yr,
                  cs, cr, es, er, ms, mr, go):
    p, i, e = place()
    z, c = e // 2, e % 2
    nz = ne // 2
    npipe = lax.axis_size("pipe")
    tokens, width = x_hbm.shape
    slots = ne * CAP
    chosen = ids.shape[0]
    hs = wg.shape[1]
    places = len(Z_PLACES)
    half = places // 2
    chip_rows = 2 * CAP
    share = half * chip_rows
    band = nd * share
    nt = (((1,), (1,)), ((), ()))
    right, left = (p, mod(i + 1, nd), e), (p, mod(i - 1, nd), e)
    sides = (right, left)
    peers = (None, right, left, (p, mod(i + 2, nd), e))
    prev, nxt = mod(p - 1, npipe), mod(p + 1, npipe)

    barrier = pltpu.get_barrier_semaphore()

    def greet(device):
        pl.semaphore_signal(barrier, inc=1, device_id=device, device_id_type=MESH)

    for d in range(1, ne):
        greet((p, i, lax.rem(e + d, ne)))
    for s in range(1, nd):
        greet(peers[s])
    greet((prev, i, e))

    loads = [pltpu.make_async_copy(a, b, lsem.at[n]) for n, (a, b) in enumerate(
        ((ids_hbm, ids), (w_hbm, wts), (x_hbm, xv), (dy_hbm, dyv), (wg_hbm, wg), (wu_hbm, wu), (wd_hbm, wd)))]
    for copy in loads:
        copy.start()
    loads[0].wait()
    loads[1].wait()

    expert, rank_of = slot_maps(ids, slots, tokens)
    hit = jnp.zeros((slots, tokens), F32)
    weight = jnp.zeros((slots, tokens), F32)
    for k in range(chosen):
        same = ids[k] == expert
        hit = jnp.where(same, 1.0, hit)
        weight = jnp.where(same, wts[k], weight)
    before = (lax.broadcasted_iota(jnp.int32, (tokens, tokens), 0)
              < lax.broadcasted_iota(jnp.int32, (tokens, tokens), 1))
    rank = jnp.dot(hit.astype(BF16), jnp.where(before, 1.0, 0.0).astype(BF16), preferred_element_type=F32)
    table = jnp.where(rank == rank_of.astype(F32), hit, 0.0)
    slot_weight = jnp.sum(table * weight, axis=1, keepdims=True)
    table = table.astype(BF16)
    smap[...] = table
    loads[2].wait()
    sx[...] = jnp.dot(table, xv[...], preferred_element_type=F32).astype(BF16)
    pl.semaphore_wait(barrier, ne - 1 + nd - 1 + 1)

    send, recv = (sx, sg), (rx, rg)

    def group(pos, slot):
        return pl.ds(pos // half * band + slot * share + pos % half * chip_rows, chip_rows)

    def core(dc):
        return c + dc - 2 * c * dc

    def z_copy(kind, pos, dc):
        target = mod(z - Z_PLACES[pos], nz) * 2 + core(dc)
        row = pos // half * band + pos % half * chip_rows
        return remote(send[kind].at[eight(target * CAP)], recv[kind].at[eight(row + c * CAP)],
                      zs.at[kind, 2 * pos + dc], zr.at[kind, 2 * pos + dc], (p, i, target))

    def own(kind):
        return pltpu.make_async_copy(send[kind].at[eight(e * CAP)], recv[kind].at[eight(c * CAP)], lsem.at[7 + kind])

    def x_copy(kind, pos, way):
        return remote(recv[kind].at[group(pos, 0)], recv[kind].at[group(pos, 2 - way)],
                      xs.at[kind, pos, way], xr.at[kind, pos, way], sides[way])

    def f_way(kind, pos):
        return (pos + kind) % 2

    def f_copy(kind, pos):
        way = f_way(kind, pos)
        return remote(recv[kind].at[group(pos, 2 - way)], recv[kind].at[group(pos, 3)],
                      fs.at[kind, pos], fr.at[kind, pos], sides[way])

    def z_send(kind, pos):
        for dc in (0, 1):
            if (pos, dc) == (0, 0):
                own(kind).start()
            else:
                z_copy(kind, pos, dc).start()

    def z_step(kind, pos):
        for dc in (0, 1):
            if (pos, dc) == (0, 0):
                own(kind).wait()
            else:
                z_copy(kind, pos, dc).wait_recv()
        for way in (0, 1):
            x_copy(kind, pos, way).start()

    def forward(kind, pos):
        x_copy(kind, pos, f_way(kind, pos)).wait_recv()
        f_copy(kind, pos).start()

    def direct_in(kind, h):
        for pos in range(h * half, (h + 1) * half):
            x_copy(kind, pos, 1 - f_way(kind, pos)).wait_recv()

    def opposite_in(kind, h):
        for pos in range(h * half, (h + 1) * half):
            f_copy(kind, pos).wait_recv()

    def map_copy():
        return remote(smap, next_hbm, ms.at[0], mr.at[0], (prev, i, e))

    def rows(h, slot, count):
        return slice(h * band + slot * share, h * band + (slot + count) * share)

    def inner(h, slot, count):
        r = rows(h, slot, count)
        gu[r, 0:hs] = jnp.dot(rx[r, :], wg[...], preferred_element_type=F32)
        gu[r, hs:] = jnp.dot(rx[r, :], wu[...], preferred_element_type=F32)

    def act(h, slot, count):
        r = rows(h, slot, count)
        n = count * share
        gate, up = gu[r, 0:hs], gu[r, hs:]
        gh = lax.dot_general(rg[r, :], wd[...], nt, preferred_element_type=F32)
        sig = jax.nn.sigmoid(gate)
        swish = gate * sig
        hidden = swish * up
        total = jnp.sum(hidden * gh, axis=1, keepdims=True)
        lane = lax.broadcasted_iota(jnp.int32, (n, 128), 1)
        row = jnp.bitwise_and(lax.broadcasted_iota(jnp.int32, (n, 128), 0), CAP - 1)
        spread = jnp.where(lane == row, jnp.broadcast_to(total, (n, 128)), 0.0)
        score[r.start // CAP:r.stop // CAP] = jnp.sum(spread.reshape(n // CAP, CAP, 128), axis=1, keepdims=True)
        hid[r, :] = hidden.astype(BF16)
        delta[r, 0:hs] = (gh * up * sig * (1.0 + gate * (1.0 - sig))).astype(BF16)
        delta[r, hs:] = (gh * swish).astype(BF16)

    def partial(h, slot, count):
        r = rows(h, slot, count)
        dg, du = delta[r, 0:hs], delta[r, hs:]
        wide = 512
        for t in range(width // wide):
            cut = slice(t * wide, (t + 1) * wide)
            value = lax.dot_general(dg, wg[cut, :], nt, preferred_element_type=F32)
            value += lax.dot_general(du, wu[cut, :], nt, preferred_element_type=F32)
            part[r, cut] = value.astype(BF16)

    def mine(h):
        return slice(h * share, (h + 1) * share)

    def cols(q):
        return slice(pieces[q][1], pieces[q][1] + pieces[q][2])

    def step1(q):
        h = pieces[q][0]
        return remote(part.at[rows(h, 3, 1), cols(q)], b1.at[mine(h), cols(q)], s1s.at[q], s1r.at[q], sides[q % 2])

    def plain(q):
        h = pieces[q][0]
        return remote(part.at[rows(h, 2 - q % 2, 1), cols(q)], bu.at[mine(h), cols(q)], sus.at[q], sur.at[q],
                      sides[1 - q % 2])

    def step2(q):
        h = pieces[q][0]
        return remote(b1.at[mine(h), cols(q)], b2.at[mine(h), cols(q)], s2s.at[q], s2r.at[q], sides[q % 2])

    def score_x(s, h):
        blocks = share // CAP
        n = (s - 1) * 2 + h
        return remote(score.at[pl.ds((h * nd + s) * blocks, blocks)], sc3.at[s - 1, pl.ds(h * blocks, blocks)],
                      cs.at[n], cr.at[n], peers[s])

    def score_z(pos, dc):
        target = mod(z + Z_PLACES[pos], nz) * 2 + core(dc)
        return remote(own_score.at[2 * pos + core(dc)], score_hbm.at[e], es.at[2 * pos + dc], er.at[2 * pos + dc],
                      (p, i, target))

    def score_own():
        return pltpu.make_async_copy(own_score.at[c], score_hbm.at[e], lsem.at[9])

    def y_copy(pair, pos, dc):
        h, start, size = pieces[2 * pair]
        wide = pl.ds(start, 2 * size)
        target = mod(z + Z_PLACES[pos], nz) * 2 + core(dc)
        n = pos % half * 2 + dc
        return remote(fin.at[eight(pos * chip_rows + core(dc) * CAP), wide], rows_hbm.at[eight(e * CAP), wide],
                      ys.at[pair, n], yr.at[pair, n], (prev, i, target))

    def all_y(pair):
        h = pieces[2 * pair][0]
        return [y_copy(pair, pos, dc) for pos in range(h * half, (h + 1) * half) for dc in (0, 1)]

    def both(copy, pair):
        for q in (2 * pair, 2 * pair + 1):
            copy(q).start()

    def middle(pair):
        for q in (2 * pair, 2 * pair + 1):
            h = pieces[q][0]
            step1(q).wait_recv()
            total = part[rows(h, 1 + q % 2, 1), cols(q)].astype(F32) + b1[mine(h), cols(q)].astype(F32)
            b1[mine(h), cols(q)] = total.astype(BF16)
            step2(q).start()

    def finish(pair):
        h = pieces[2 * pair][0]
        for q in (2 * pair, 2 * pair + 1):
            plain(q).wait_recv()
            step2(q).wait_recv()
            total = (part[rows(h, 0, 1), cols(q)].astype(F32) + b2[mine(h), cols(q)].astype(F32)
                     + bu[mine(h), cols(q)].astype(F32))
            fin[mine(h), cols(q)] = total.astype(BF16)
        for copy in all_y(pair):
            copy.start()

    first, second = len(PAIRS[0]), len(PAIRS[1])

    for pos in range(LOOK):
        z_send(0, pos)
    loads[3].wait()
    sg[...] = (slot_weight * jnp.dot(table, dyv[...], preferred_element_type=F32)).astype(BF16)
    for pos in range(LOOK):
        z_send(1, pos)
    pl.semaphore_signal(go, inc=1, device_id=(nxt, i, e), device_id_type=MESH)
    for copy in loads[4:]:
        copy.wait()
    steps = [(kind, pos) for pos in range(places) for kind in (0, 1)]
    for t, (kind, pos) in enumerate(steps):
        z_step(kind, pos)
        if kind == 1 and pos + LOOK < places:
            z_send(0, pos + LOOK)
            z_send(1, pos + LOOK)
        if t >= LAG:
            forward(*steps[t - LAG])
        if t == 13:
            direct_in(0, 0)
            opposite_in(0, 0)
            inner(0, 0, nd)
    forward(*steps[12])
    direct_in(1, 0)
    opposite_in(1, 0)
    act(0, 0, nd)
    forward(*steps[13])
    forward(*steps[14])
    partial(0, 1, nd - 1)
    forward(*steps[15])
    for pair in range(first):
        both(step1, pair)
        both(plain, pair)
    pl.semaphore_wait(go, 1)
    map_copy().start()
    partial(0, 0, 1)
    direct_in(0, 1)
    inner(1, 0, nd - 1)
    middle(0)
    direct_in(1, 1)
    act(1, 0, nd - 1)
    for pair in range(1, first):
        middle(pair)
    partial(1, 1, 2)
    both(plain, first)
    both(plain, first + 1)
    opposite_in(0, 1)
    inner(1, 3, 1)
    opposite_in(1, 1)
    act(1, 3, 1)
    partial(1, 3, 1)
    both(step1, first)
    both(step1, first + 1)
    for s in range(1, nd):
        for h in (0, 1):
            score_x(s, h).start()
    for pair in range(first):
        finish(pair)
    partial(1, 0, 1)
    middle(first)
    for pair in range(first + 2, first + second):
        both(step1, pair)
        both(plain, pair)
    middle(first + 1)
    finish(first)
    for s in range(1, nd):
        for h in (0, 1):
            score_x(s, h).wait_recv()
    blocks = share // CAP
    for h in (0, 1):
        here = slice(h * blocks, (h + 1) * blocks)
        own_score[here] = (score[h * nd * blocks:h * nd * blocks + blocks]
                           + sc3[0, here] + sc3[1, here] + sc3[2, here])
    score_own().start()
    for pos in range(places):
        for dc in (0, 1):
            if (pos, dc) != (0, 0):
                score_z(pos, dc).start()
    saves = [pltpu.make_async_copy(a, b, lsem.at[10 + n]) for n, (a, b) in enumerate(
        ((rx, rx_hbm), (rg, rg_hbm), (delta, delta_hbm), (hid, hidden_hbm), (smap, smap_hbm)))]
    for copy in saves:
        copy.start()
    for pair in range(first + 2, first + second):
        middle(pair)
        finish(pair - 1)
    finish(first + second - 1)

    for copy in saves:
        copy.wait()
    for kind in (0, 1):
        for pos in range(places):
            for dc in (0, 1):
                if (pos, dc) != (0, 0):
                    z_copy(kind, pos, dc).wait_send()
            for way in (0, 1):
                x_copy(kind, pos, way).wait_send()
            f_copy(kind, pos).wait_send()
    for q in range(len(pieces)):
        step1(q).wait_send()
        plain(q).wait_send()
        step2(q).wait_send()
    map_copy().wait_send()
    map_copy().wait_recv()
    score_own().wait()
    for s in range(1, nd):
        for h in (0, 1):
            score_x(s, h).wait_send()
    for pos in range(places):
        for dc in (0, 1):
            if (pos, dc) != (0, 0):
                score_z(pos, dc).wait_send()
                score_z(pos, dc).wait_recv()
    for pair in range(len(pieces) // 2):
        for copy in all_y(pair):
            copy.wait_send()
            copy.wait_recv()


def routed(acts, grads, ids, weights, wg, wu, wd, nd, ne):
    tokens, width = acts.shape
    hs = wg.shape[1]
    slots = ne * CAP
    rows = nd * slots
    pieces = []
    for h, sizes in enumerate(PAIRS):
        start = 0
        for size in sizes:
            pieces += [(h, start, size // 2), (h, start + size // 2, size // 2)]
            start += size
    hbm = pl.BlockSpec(memory_space=pltpu.HBM)
    dma = pltpu.SemaphoreType.DMA
    places, n = len(Z_PLACES), len(pieces)
    shape = jax.ShapeDtypeStruct
    block = pltpu.VMEM((slots, width), BF16)
    full = pltpu.VMEM((rows, width), BF16)
    return pl.pallas_call(
        functools.partial(routed_kernel, nd, ne, pieces),
        out_shape=(shape((slots, width), BF16), shape((slots, tokens), BF16), shape((ne, 1, 128), F32),
                   shape((slots, tokens), BF16), shape((rows, width), BF16), shape((rows, width), BF16),
                   shape((rows, 2 * hs), BF16), shape((rows, hs), BF16)),
        in_specs=[hbm] * 7,
        out_specs=(hbm,) * 8,
        scratch_shapes=[pltpu.VMEM((tokens, width), BF16), pltpu.VMEM((tokens, width), BF16),
                        pltpu.VMEM(ids.shape, jnp.int32), pltpu.VMEM(ids.shape, F32), pltpu.VMEM((slots, tokens), BF16),
                        block, block, full, full, pltpu.VMEM(wg.shape, BF16), pltpu.VMEM(wu.shape, BF16),
                        pltpu.VMEM(wd.shape, BF16), pltpu.VMEM((rows, 2 * hs), F32), pltpu.VMEM((rows, 2 * hs), BF16),
                        pltpu.VMEM((rows, hs), BF16), full, block, block, block, block,
                        pltpu.VMEM((nd * ne, 1, 128), F32), pltpu.VMEM((nd - 1, ne, 1, 128), F32),
                        pltpu.VMEM((ne, 1, 128), F32),
                        dma((15,)), dma((2, ne)), dma((2, ne)), dma((2, places, 2)), dma((2, places, 2)),
                        dma((2, places)), dma((2, places))] + [dma((n,))] * 6 + [dma((n // 2, ne // 2))] * 2
        + [dma((2 * (nd - 1),))] * 2 + [dma((ne,))] * 2 + [dma((1,))] * 2 + [pltpu.SemaphoreType.REGULAR],
        compiler_params=pltpu.CompilerParams(collective_id=0, has_side_effects=True, vmem_limit_bytes=VMEM_LIMIT),
        name="routed",
    )(acts, grads, ids, weights, wg, wu, wd)


def local_kernel(rx, rg, delta, hid, rows, snext, smap, score, ids_ref, w_ref, out, gwg, dwg, dwu, dwd):
    tn = (((0,), (0,)), ((), ()))
    hs = hid.shape[1]
    slots, tokens = smap.shape

    @pl.when(pl.program_id(0) == 0)
    def _():
        ne = slots // CAP
        column = jnp.broadcast_to(score[...], (ne, CAP, 128)).reshape(slots, 128)
        expert, _ = slot_maps(ids_ref, slots, tokens)
        lane = lax.broadcasted_iota(jnp.int32, (slots, 128), 1)
        row = jnp.bitwise_and(lax.broadcasted_iota(jnp.int32, (slots, 128), 0), CAP - 1)
        column = jnp.sum(jnp.where(lane == row, column, 0.0), axis=1, keepdims=True)
        spread = smap[...].astype(F32) * column
        for k in range(ids_ref.shape[0]):
            picked = jnp.sum(jnp.where(ids_ref[k] == expert, spread, 0.0), axis=0, keepdims=True)
            gwg[k] = picked / w_ref[k]

    out[...] = lax.dot_general(snext[...], rows[...], tn, preferred_element_type=F32).astype(BF16)
    both = lax.dot_general(rx[...], delta[...], tn, preferred_element_type=F32).astype(BF16)
    dwg[...] = both[:, :hs]
    dwu[...] = both[:, hs:]
    dwd[...] = lax.dot_general(hid[...], rg[...], tn, preferred_element_type=F32).astype(BF16)


def local(rows, snext, score, smap, rx, rg, delta, hid, ids, weights):
    count, width = rx.shape
    hs = hid.shape[1]
    slots, tokens = smap.shape
    wide = 512

    def whole(array):
        return pl.BlockSpec(array.shape, lambda t: (0,) * array.ndim)

    def across(height):
        return pl.BlockSpec((height, wide), lambda t: (0, t))

    down = pl.BlockSpec((wide, hs), lambda t: (t, 0))
    shape = jax.ShapeDtypeStruct
    return pl.pallas_call(
        local_kernel,
        grid=(width // wide,),
        out_shape=(shape((tokens, width), BF16), shape(ids.shape, F32), shape((width, hs), BF16),
                   shape((width, hs), BF16), shape((hs, width), BF16)),
        in_specs=[across(count), across(count), whole(delta), whole(hid), across(slots), whole(snext), whole(smap),
                  whole(score), whole(ids), whole(weights)],
        out_specs=(across(tokens), whole(ids), down, down, across(hs)),
        compiler_params=pltpu.CompilerParams(vmem_limit_bytes=VMEM_LIMIT),
        name="local",
    )(rx, rg, delta, hid, rows, snext, smap, score, ids, weights)


def shards(block_input, output_grad, expert_ids, gate_weights, gate_proj, up_proj, down_proj):
    nd, ne = lax.axis_size("dp"), lax.axis_size("expert")
    ids = jnp.transpose(expert_ids, (2, 0, 1))
    weights = jnp.transpose(gate_weights, (2, 0, 1))
    outs = routed(block_input[0], output_grad[0], ids, weights, gate_proj[0, 0], up_proj[0, 0], down_proj[0, 0],
                  nd, ne)
    received, gwg, dwg, dwu, dwd = local(*outs, ids, weights)
    return (received[None], jnp.transpose(gwg, (1, 2, 0)), dwg[None, None], dwu[None, None], dwd[None, None])


def solution(mesh):
    in_specs = (
        P("pipe", ("dp", "expert"), None),
        P("pipe", ("dp", "expert"), None),
        P("pipe", ("dp", "expert"), None),
        P("pipe", ("dp", "expert"), None),
        P("pipe", "expert", None, "dp"),
        P("pipe", "expert", None, "dp"),
        P("pipe", "expert", "dp", None),
    )
    out_specs = (
        P("pipe", ("dp", "expert"), None),
        P("pipe", ("dp", "expert"), None),
        P("pipe", "expert", None, "dp"),
        P("pipe", "expert", None, "dp"),
        P("pipe", "expert", "dp", None),
    )
    return jax.shard_map(shards, mesh=mesh, in_specs=in_specs, out_specs=out_specs, check_vma=False)
```

```python
import functools
import jax
import jax.numpy as jnp
from jax import lax
from jax.experimental import pallas as pl
from jax.experimental.pallas import tpu as pltpu
from jax.sharding import PartitionSpec as P

MESH = pl.DeviceIdType.MESH
CAP = 8
F32 = jnp.float32
BF16 = jnp.bfloat16
VMEM_LIMIT = 58 << 20
Z_PLACES = (0, 1, -1, 2, -2, 3, -3, 4)
LOOK = 2
LAG = 4
PAIRS = ((1536, 1536), (1280, 1024, 768))


def mod(value, count):
    return lax.rem(value + count, count)


def place():
    return lax.axis_index("pipe"), lax.axis_index("dp"), lax.axis_index("expert")


def remote(src, dst, send_sem, recv_sem, device):
    return pltpu.make_async_remote_copy(
        src_ref=src, dst_ref=dst, send_sem=send_sem, recv_sem=recv_sem,
        device_id=device, device_id_type=MESH)


def eight(row):
    return pl.ds(pl.multiple_of(row, 8), 8)


def slot_maps(ids_ref, slots, tokens):
    slot = lax.broadcasted_iota(jnp.int32, (slots, tokens), 0)
    expert = lax.shift_right_logical(slot, 3)
    rank = jnp.bitwise_and(slot, 7)
    return expert, rank


def routed_kernel(nd, ne, pieces, x_hbm, dy_hbm, ids_hbm, w_hbm, wg_hbm, wu_hbm, wd_hbm,
                  rows_hbm, next_hbm, score_hbm, smap_hbm, rx_hbm, rg_hbm, delta_hbm, hidden_hbm,
                  xv, dyv, ids, wts, smap, sx, sg, rx, rg, wg, wu, wd, gu, delta, hid, part, b1, b2, bu, fin,
                  score, sc3, own_score, lsem, zs, zr, xs, xr, fs, fr, s1s, s1r, s2s, s2r, sus, sur, ys, yr,
                  cs, cr, es, er, ms, mr, go):
    p, i, e = place()
    z, c = e // 2, e % 2
    nz = ne // 2
    npipe = lax.axis_size("pipe")
    tokens, width = x_hbm.shape
    slots = ne * CAP
    chosen = ids.shape[0]
    hs = wg.shape[1]
    places = len(Z_PLACES)
    half = places // 2
    chip_rows = 2 * CAP
    share = half * chip_rows
    band = nd * share
    nt = (((1,), (1,)), ((), ()))
    right, left = (p, mod(i + 1, nd), e), (p, mod(i - 1, nd), e)
    sides = (right, left)
    peers = (None, right, left, (p, mod(i + 2, nd), e))
    prev, nxt = mod(p - 1, npipe), mod(p + 1, npipe)

    barrier = pltpu.get_barrier_semaphore()

    def greet(device):
        pl.semaphore_signal(barrier, inc=1, device_id=device, device_id_type=MESH)

    for d in range(1, ne):
        greet((p, i, lax.rem(e + d, ne)))
    for s in range(1, nd):
        greet(peers[s])
    greet((prev, i, e))

    loads = [pltpu.make_async_copy(a, b, lsem.at[n]) for n, (a, b) in enumerate(
        ((ids_hbm, ids), (w_hbm, wts), (x_hbm, xv), (dy_hbm, dyv), (wg_hbm, wg), (wu_hbm, wu), (wd_hbm, wd)))]
    for copy in loads:
        copy.start()
    loads[0].wait()
    loads[1].wait()

    expert, rank_of = slot_maps(ids, slots, tokens)
    hit = jnp.zeros((slots, tokens), F32)
    weight = jnp.zeros((slots, tokens), F32)
    for k in range(chosen):
        same = ids[k] == expert
        hit = jnp.where(same, 1.0, hit)
        weight = jnp.where(same, wts[k], weight)
    before = (lax.broadcasted_iota(jnp.int32, (tokens, tokens), 0)
              < lax.broadcasted_iota(jnp.int32, (tokens, tokens), 1))
    rank = jnp.dot(hit.astype(BF16), jnp.where(before, 1.0, 0.0).astype(BF16), preferred_element_type=F32)
    table = jnp.where(rank == rank_of.astype(F32), hit, 0.0)
    slot_weight = jnp.sum(table * weight, axis=1, keepdims=True)
    table = table.astype(BF16)
    smap[...] = table
    loads[2].wait()
    sx[...] = jnp.dot(table, xv[...], preferred_element_type=F32).astype(BF16)
    pl.semaphore_wait(barrier, ne - 1 + nd - 1 + 1)

    send, recv = (sx, sg), (rx, rg)

    def group(pos, slot):
        return pl.ds(pos // half * band + slot * share + pos % half * chip_rows, chip_rows)

    def core(dc):
        return c + dc - 2 * c * dc

    def z_copy(kind, pos, dc):
        target = mod(z - Z_PLACES[pos], nz) * 2 + core(dc)
        row = pos // half * band + pos % half * chip_rows
        return remote(send[kind].at[eight(target * CAP)], recv[kind].at[eight(row + c * CAP)],
                      zs.at[kind, 2 * pos + dc], zr.at[kind, 2 * pos + dc], (p, i, target))

    def own(kind):
        return pltpu.make_async_copy(send[kind].at[eight(e * CAP)], recv[kind].at[eight(c * CAP)], lsem.at[7 + kind])

    def x_copy(kind, pos, way):
        return remote(recv[kind].at[group(pos, 0)], recv[kind].at[group(pos, 2 - way)],
                      xs.at[kind, pos, way], xr.at[kind, pos, way], sides[way])

    def f_way(kind, pos):
        return (pos + kind) % 2

    def f_copy(kind, pos):
        way = f_way(kind, pos)
        return remote(recv[kind].at[group(pos, 2 - way)], recv[kind].at[group(pos, 3)],
                      fs.at[kind, pos], fr.at[kind, pos], sides[way])

    def z_send(kind, pos):
        for dc in (0, 1):
            if (pos, dc) == (0, 0):
                own(kind).start()
            else:
                z_copy(kind, pos, dc).start()

    def z_step(kind, pos):
        for dc in (0, 1):
            if (pos, dc) == (0, 0):
                own(kind).wait()
            else:
                z_copy(kind, pos, dc).wait_recv()
        for way in (0, 1):
            x_copy(kind, pos, way).start()

    def forward(kind, pos):
        x_copy(kind, pos, f_way(kind, pos)).wait_recv()
        f_copy(kind, pos).start()

    def direct_in(kind, h):
        for pos in range(h * half, (h + 1) * half):
            x_copy(kind, pos, 1 - f_way(kind, pos)).wait_recv()

    def opposite_in(kind, h):
        for pos in range(h * half, (h + 1) * half):
            f_copy(kind, pos).wait_recv()

    def map_copy():
        return remote(smap, next_hbm, ms.at[0], mr.at[0], (prev, i, e))

    def rows(h, slot, count):
        return slice(h * band + slot * share, h * band + (slot + count) * share)

    def inner(h, slot, count):
        r = rows(h, slot, count)
        gu[r, 0:hs] = jnp.dot(rx[r, :], wg[...], preferred_element_type=F32)
        gu[r, hs:] = jnp.dot(rx[r, :], wu[...], preferred_element_type=F32)

    def act(h, slot, count):
        r = rows(h, slot, count)
        n = count * share
        gate, up = gu[r, 0:hs], gu[r, hs:]
        gh = lax.dot_general(rg[r, :], wd[...], nt, preferred_element_type=F32)
        sig = jax.nn.sigmoid(gate)
        swish = gate * sig
        hidden = swish * up
        total = jnp.sum(hidden * gh, axis=1, keepdims=True)
        lane = lax.broadcasted_iota(jnp.int32, (n, 128), 1)
        row = jnp.bitwise_and(lax.broadcasted_iota(jnp.int32, (n, 128), 0), CAP - 1)
        spread = jnp.where(lane == row, jnp.broadcast_to(total, (n, 128)), 0.0)
        score[r.start // CAP:r.stop // CAP] = jnp.sum(spread.reshape(n // CAP, CAP, 128), axis=1, keepdims=True)
        hid[r, :] = hidden.astype(BF16)
        delta[r, 0:hs] = (gh * up * sig * (1.0 + gate * (1.0 - sig))).astype(BF16)
        delta[r, hs:] = (gh * swish).astype(BF16)

    def partial(h, slot, count):
        r = rows(h, slot, count)
        dg, du = delta[r, 0:hs], delta[r, hs:]
        wide = 512
        for t in range(width // wide):
            cut = slice(t * wide, (t + 1) * wide)
            value = lax.dot_general(dg, wg[cut, :], nt, preferred_element_type=F32)
            value += lax.dot_general(du, wu[cut, :], nt, preferred_element_type=F32)
            part[r, cut] = value.astype(BF16)

    def mine(h):
        return slice(h * share, (h + 1) * share)

    def cols(q):
        return slice(pieces[q][1], pieces[q][1] + pieces[q][2])

    def step1(q):
        h = pieces[q][0]
        return remote(part.at[rows(h, 3, 1), cols(q)], b1.at[mine(h), cols(q)], s1s.at[q], s1r.at[q], sides[q % 2])

    def plain(q):
        h = pieces[q][0]
        return remote(part.at[rows(h, 2 - q % 2, 1), cols(q)], bu.at[mine(h), cols(q)], sus.at[q], sur.at[q],
                      sides[1 - q % 2])

    def step2(q):
        h = pieces[q][0]
        return remote(b1.at[mine(h), cols(q)], b2.at[mine(h), cols(q)], s2s.at[q], s2r.at[q], sides[q % 2])

    def score_x(s, h):
        blocks = share // CAP
        n = (s - 1) * 2 + h
        return remote(score.at[pl.ds((h * nd + s) * blocks, blocks)], sc3.at[s - 1, pl.ds(h * blocks, blocks)],
                      cs.at[n], cr.at[n], peers[s])

    def score_z(pos, dc):
        target = mod(z + Z_PLACES[pos], nz) * 2 + core(dc)
        return remote(own_score.at[2 * pos + core(dc)], score_hbm.at[e], es.at[2 * pos + dc], er.at[2 * pos + dc],
                      (p, i, target))

    def score_own():
        return pltpu.make_async_copy(own_score.at[c], score_hbm.at[e], lsem.at[9])

    def y_copy(pair, pos, dc):
        h, start, size = pieces[2 * pair]
        wide = pl.ds(start, 2 * size)
        target = mod(z + Z_PLACES[pos], nz) * 2 + core(dc)
        n = pos % half * 2 + dc
        return remote(fin.at[eight(pos * chip_rows + core(dc) * CAP), wide], rows_hbm.at[eight(e * CAP), wide],
                      ys.at[pair, n], yr.at[pair, n], (prev, i, target))

    def all_y(pair):
        h = pieces[2 * pair][0]
        return [y_copy(pair, pos, dc) for pos in range(h * half, (h + 1) * half) for dc in (0, 1)]

    def both(copy, pair):
        for q in (2 * pair, 2 * pair + 1):
            copy(q).start()

    def middle(pair):
        for q in (2 * pair, 2 * pair + 1):
            h = pieces[q][0]
            step1(q).wait_recv()
            total = part[rows(h, 1 + q % 2, 1), cols(q)].astype(F32) + b1[mine(h), cols(q)].astype(F32)
            b1[mine(h), cols(q)] = total.astype(BF16)
            step2(q).start()

    def finish(pair):
        h = pieces[2 * pair][0]
        for q in (2 * pair, 2 * pair + 1):
            plain(q).wait_recv()
            step2(q).wait_recv()
            total = (part[rows(h, 0, 1), cols(q)].astype(F32) + b2[mine(h), cols(q)].astype(F32)
                     + bu[mine(h), cols(q)].astype(F32))
            fin[mine(h), cols(q)] = total.astype(BF16)
        for copy in all_y(pair):
            copy.start()

    first, second = len(PAIRS[0]), len(PAIRS[1])

    for pos in range(LOOK):
        z_send(0, pos)
    loads[3].wait()
    sg[...] = (slot_weight * jnp.dot(table, dyv[...], preferred_element_type=F32)).astype(BF16)
    for pos in range(LOOK):
        z_send(1, pos)
    pl.semaphore_signal(go, inc=1, device_id=(nxt, i, e), device_id_type=MESH)
    for copy in loads[4:]:
        copy.wait()
    steps = [(kind, pos) for pos in range(places) for kind in (0, 1)]
    for t, (kind, pos) in enumerate(steps):
        z_step(kind, pos)
        if kind == 1 and pos + LOOK < places:
            z_send(0, pos + LOOK)
            z_send(1, pos + LOOK)
        if t >= LAG:
            forward(*steps[t - LAG])
        if t == 11:
            direct_in(0, 0)
            opposite_in(0, 0)
            inner(0, 0, nd)
        if t == 12:
            direct_in(1, 0)
            opposite_in(1, 0)
            act(0, 0, nd)
        if t == 14:
            partial(0, 3, 1)
            for pair in range(first):
                both(step1, pair)
    forward(*steps[12])
    forward(*steps[13])
    partial(0, 1, 2)
    forward(*steps[14])
    forward(*steps[15])
    middle(0)
    both(plain, 0)
    for pair in range(1, first):
        middle(pair)
        both(plain, pair)
    pl.semaphore_wait(go, 1)
    map_copy().start()
    partial(0, 0, 1)
    direct_in(0, 1)
    inner(1, 0, nd - 1)
    opposite_in(0, 1)
    inner(1, 3, 1)
    direct_in(1, 1)
    act(1, 0, nd - 1)
    opposite_in(1, 1)
    act(1, 3, 1)
    partial(1, 3, 1)
    for pair in range(first, first + second):
        both(step1, pair)
    partial(1, 1, 2)
    both(plain, first)
    for s in range(1, nd):
        for h in (0, 1):
            score_x(s, h).start()
    saves = [pltpu.make_async_copy(a, b, lsem.at[10 + n]) for n, (a, b) in enumerate(
        ((rx, rx_hbm), (rg, rg_hbm), (delta, delta_hbm), (hid, hidden_hbm), (smap, smap_hbm)))]
    for copy in saves:
        copy.start()
    partial(1, 0, 1)
    for pair in range(first):
        finish(pair)
    for pair in range(first, first + second):
        middle(pair)
        if pair + 1 < first + second:
            both(plain, pair + 1)
    finish(first)
    for s in range(1, nd):
        for h in (0, 1):
            score_x(s, h).wait_recv()
    blocks = share // CAP
    for h in (0, 1):
        here = slice(h * blocks, (h + 1) * blocks)
        own_score[here] = (score[h * nd * blocks:h * nd * blocks + blocks]
                           + sc3[0, here] + sc3[1, here] + sc3[2, here])
    score_own().start()
    for pos in range(places):
        for dc in (0, 1):
            if (pos, dc) != (0, 0):
                score_z(pos, dc).start()
    for pair in range(first + 1, first + second):
        finish(pair)

    for copy in saves:
        copy.wait()
    for kind in (0, 1):
        for pos in range(places):
            for dc in (0, 1):
                if (pos, dc) != (0, 0):
                    z_copy(kind, pos, dc).wait_send()
            for way in (0, 1):
                x_copy(kind, pos, way).wait_send()
            f_copy(kind, pos).wait_send()
    for q in range(len(pieces)):
        step1(q).wait_send()
        plain(q).wait_send()
        step2(q).wait_send()
    map_copy().wait_send()
    map_copy().wait_recv()
    score_own().wait()
    for s in range(1, nd):
        for h in (0, 1):
            score_x(s, h).wait_send()
    for pos in range(places):
        for dc in (0, 1):
            if (pos, dc) != (0, 0):
                score_z(pos, dc).wait_send()
                score_z(pos, dc).wait_recv()
    for pair in range(len(pieces) // 2):
        for copy in all_y(pair):
            copy.wait_send()
            copy.wait_recv()


def routed(acts, grads, ids, weights, wg, wu, wd, nd, ne):
    tokens, width = acts.shape
    hs = wg.shape[1]
    slots = ne * CAP
    rows = nd * slots
    pieces = []
    for h, sizes in enumerate(PAIRS):
        start = 0
        for size in sizes:
            pieces += [(h, start, size // 2), (h, start + size // 2, size // 2)]
            start += size
    hbm = pl.BlockSpec(memory_space=pltpu.HBM)
    dma = pltpu.SemaphoreType.DMA
    places, n = len(Z_PLACES), len(pieces)
    shape = jax.ShapeDtypeStruct
    block = pltpu.VMEM((slots, width), BF16)
    full = pltpu.VMEM((rows, width), BF16)
    return pl.pallas_call(
        functools.partial(routed_kernel, nd, ne, pieces),
        out_shape=(shape((slots, width), BF16), shape((slots, tokens), BF16), shape((ne, 1, 128), F32),
                   shape((slots, tokens), BF16), shape((rows, width), BF16), shape((rows, width), BF16),
                   shape((rows, 2 * hs), BF16), shape((rows, hs), BF16)),
        in_specs=[hbm] * 7,
        out_specs=(hbm,) * 8,
        scratch_shapes=[pltpu.VMEM((tokens, width), BF16), pltpu.VMEM((tokens, width), BF16),
                        pltpu.VMEM(ids.shape, jnp.int32), pltpu.VMEM(ids.shape, F32), pltpu.VMEM((slots, tokens), BF16),
                        block, block, full, full, pltpu.VMEM(wg.shape, BF16), pltpu.VMEM(wu.shape, BF16),
                        pltpu.VMEM(wd.shape, BF16), pltpu.VMEM((rows, 2 * hs), F32), pltpu.VMEM((rows, 2 * hs), BF16),
                        pltpu.VMEM((rows, hs), BF16), full, block, block, block, block,
                        pltpu.VMEM((nd * ne, 1, 128), F32), pltpu.VMEM((nd - 1, ne, 1, 128), F32),
                        pltpu.VMEM((ne, 1, 128), F32),
                        dma((15,)), dma((2, ne)), dma((2, ne)), dma((2, places, 2)), dma((2, places, 2)),
                        dma((2, places)), dma((2, places))] + [dma((n,))] * 6 + [dma((n // 2, ne // 2))] * 2
        + [dma((2 * (nd - 1),))] * 2 + [dma((ne,))] * 2 + [dma((1,))] * 2 + [pltpu.SemaphoreType.REGULAR],
        compiler_params=pltpu.CompilerParams(collective_id=0, has_side_effects=True, vmem_limit_bytes=VMEM_LIMIT),
        name="routed",
    )(acts, grads, ids, weights, wg, wu, wd)


def local_kernel(rx, rg, delta, hid, rows, snext, smap, score, ids_ref, w_ref, out, gwg, dwg, dwu, dwd):
    tn = (((0,), (0,)), ((), ()))
    hs = hid.shape[1]
    slots, tokens = smap.shape

    @pl.when(pl.program_id(0) == 0)
    def _():
        ne = slots // CAP
        column = jnp.broadcast_to(score[...], (ne, CAP, 128)).reshape(slots, 128)
        expert, _ = slot_maps(ids_ref, slots, tokens)
        lane = lax.broadcasted_iota(jnp.int32, (slots, 128), 1)
        row = jnp.bitwise_and(lax.broadcasted_iota(jnp.int32, (slots, 128), 0), CAP - 1)
        column = jnp.sum(jnp.where(lane == row, column, 0.0), axis=1, keepdims=True)
        spread = smap[...].astype(F32) * column
        for k in range(ids_ref.shape[0]):
            picked = jnp.sum(jnp.where(ids_ref[k] == expert, spread, 0.0), axis=0, keepdims=True)
            gwg[k] = picked / w_ref[k]

    out[...] = lax.dot_general(snext[...], rows[...], tn, preferred_element_type=F32).astype(BF16)
    both = lax.dot_general(rx[...], delta[...], tn, preferred_element_type=F32).astype(BF16)
    dwg[...] = both[:, :hs]
    dwu[...] = both[:, hs:]
    dwd[...] = lax.dot_general(hid[...], rg[...], tn, preferred_element_type=F32).astype(BF16)


def local(rows, snext, score, smap, rx, rg, delta, hid, ids, weights):
    count, width = rx.shape
    hs = hid.shape[1]
    slots, tokens = smap.shape
    wide = 768

    def whole(array):
        return pl.BlockSpec(array.shape, lambda t: (0,) * array.ndim)

    def across(height):
        return pl.BlockSpec((height, wide), lambda t: (0, t))

    down = pl.BlockSpec((wide, hs), lambda t: (t, 0))
    shape = jax.ShapeDtypeStruct
    return pl.pallas_call(
        local_kernel,
        grid=(width // wide,),
        out_shape=(shape((tokens, width), BF16), shape(ids.shape, F32), shape((width, hs), BF16),
                   shape((width, hs), BF16), shape((hs, width), BF16)),
        in_specs=[across(count), across(count), whole(delta), whole(hid), across(slots), whole(snext), whole(smap),
                  whole(score), whole(ids), whole(weights)],
        out_specs=(across(tokens), whole(ids), down, down, across(hs)),
        compiler_params=pltpu.CompilerParams(vmem_limit_bytes=VMEM_LIMIT),
        name="local",
    )(rx, rg, delta, hid, rows, snext, smap, score, ids, weights)


def shards(block_input, output_grad, expert_ids, gate_weights, gate_proj, up_proj, down_proj):
    nd, ne = lax.axis_size("dp"), lax.axis_size("expert")
    ids = jnp.transpose(expert_ids, (2, 0, 1))
    weights = jnp.transpose(gate_weights, (2, 0, 1))
    outs = routed(block_input[0], output_grad[0], ids, weights, gate_proj[0, 0], up_proj[0, 0], down_proj[0, 0],
                  nd, ne)
    received, gwg, dwg, dwu, dwd = local(*outs, ids, weights)
    return (received[None], jnp.transpose(gwg, (1, 2, 0)), dwg[None, None], dwu[None, None], dwd[None, None])


def solution(mesh):
    in_specs = (
        P("pipe", ("dp", "expert"), None),
        P("pipe", ("dp", "expert"), None),
        P("pipe", ("dp", "expert"), None),
        P("pipe", ("dp", "expert"), None),
        P("pipe", "expert", None, "dp"),
        P("pipe", "expert", None, "dp"),
        P("pipe", "expert", "dp", None),
    )
    out_specs = (
        P("pipe", ("dp", "expert"), None),
        P("pipe", ("dp", "expert"), None),
        P("pipe", "expert", None, "dp"),
        P("pipe", "expert", None, "dp"),
        P("pipe", "expert", "dp", None),
    )
    return jax.shard_map(shards, mesh=mesh, in_specs=in_specs, out_specs=out_specs, check_vma=False)
```

```python
import functools
import jax
import jax.numpy as jnp
from jax import lax
from jax.experimental import pallas as pl
from jax.experimental.pallas import tpu as pltpu
from jax.sharding import PartitionSpec as P

MESH = pl.DeviceIdType.MESH
CAP = 8
F32 = jnp.float32
BF16 = jnp.bfloat16
VMEM_LIMIT = 58 << 20
Z_PLACES = (0, 1, -1, 4, 2, -2, 3, -3)
LOOK = 2
LAG = 4
PAIRS = ((1536, 1536), (1280, 1024, 768))


def mod(value, count):
    return lax.rem(value + count, count)


def place():
    return lax.axis_index("pipe"), lax.axis_index("dp"), lax.axis_index("expert")


def remote(src, dst, send_sem, recv_sem, device):
    return pltpu.make_async_remote_copy(
        src_ref=src, dst_ref=dst, send_sem=send_sem, recv_sem=recv_sem,
        device_id=device, device_id_type=MESH)


def eight(row):
    return pl.ds(pl.multiple_of(row, 8), 8)


def slot_maps(ids_ref, slots, tokens):
    slot = lax.broadcasted_iota(jnp.int32, (slots, tokens), 0)
    expert = lax.shift_right_logical(slot, 3)
    rank = jnp.bitwise_and(slot, 7)
    return expert, rank


def routed_kernel(nd, ne, pieces, x_hbm, dy_hbm, ids_hbm, w_hbm, wg_hbm, wu_hbm, wd_hbm,
                  rows_hbm, next_hbm, score_hbm, smap_hbm, rx_hbm, rg_hbm, delta_hbm, hidden_hbm,
                  xv, dyv, ids, wts, smap, sx, sg, rx, rg, wg, wu, wd, gu, delta, hid, part, b1, b2, bu, fin,
                  score, sc3, own_score, lsem, zs, zr, xs, xr, fs, fr, s1s, s1r, s2s, s2r, sus, sur, ys, yr,
                  cs, cr, es, er, ms, mr, go):
    p, i, e = place()
    z, c = e // 2, e % 2
    nz = ne // 2
    npipe = lax.axis_size("pipe")
    tokens, width = x_hbm.shape
    slots = ne * CAP
    chosen = ids.shape[0]
    hs = wg.shape[1]
    places = len(Z_PLACES)
    half = places // 2
    chip_rows = 2 * CAP
    share = half * chip_rows
    band = nd * share
    nt = (((1,), (1,)), ((), ()))
    right, left = (p, mod(i + 1, nd), e), (p, mod(i - 1, nd), e)
    sides = (right, left)
    peers = (None, right, left, (p, mod(i + 2, nd), e))
    prev, nxt = mod(p - 1, npipe), mod(p + 1, npipe)

    barrier = pltpu.get_barrier_semaphore()

    def greet(device):
        pl.semaphore_signal(barrier, inc=1, device_id=device, device_id_type=MESH)

    for d in range(1, ne):
        greet((p, i, lax.rem(e + d, ne)))
    for s in range(1, nd):
        greet(peers[s])
    greet((prev, i, e))

    loads = [pltpu.make_async_copy(a, b, lsem.at[n]) for n, (a, b) in enumerate(
        ((ids_hbm, ids), (w_hbm, wts), (x_hbm, xv), (dy_hbm, dyv), (wg_hbm, wg), (wu_hbm, wu), (wd_hbm, wd)))]
    for copy in loads:
        copy.start()
    loads[0].wait()
    loads[1].wait()

    expert, rank_of = slot_maps(ids, slots, tokens)
    hit = jnp.zeros((slots, tokens), F32)
    weight = jnp.zeros((slots, tokens), F32)
    for k in range(chosen):
        same = ids[k] == expert
        hit = jnp.where(same, 1.0, hit)
        weight = jnp.where(same, wts[k], weight)
    before = (lax.broadcasted_iota(jnp.int32, (tokens, tokens), 0)
              < lax.broadcasted_iota(jnp.int32, (tokens, tokens), 1))
    rank = jnp.dot(hit.astype(BF16), jnp.where(before, 1.0, 0.0).astype(BF16), preferred_element_type=F32)
    table = jnp.where(rank == rank_of.astype(F32), hit, 0.0)
    slot_weight = jnp.sum(table * weight, axis=1, keepdims=True)
    table = table.astype(BF16)
    smap[...] = table
    loads[2].wait()
    sx[...] = jnp.dot(table, xv[...], preferred_element_type=F32).astype(BF16)
    pl.semaphore_wait(barrier, ne - 1 + nd - 1 + 1)

    send, recv = (sx, sg), (rx, rg)

    def group(pos, slot):
        return pl.ds(pos // half * band + slot * share + pos % half * chip_rows, chip_rows)

    def core(dc):
        return c + dc - 2 * c * dc

    def z_copy(kind, pos, dc):
        target = mod(z - Z_PLACES[pos], nz) * 2 + core(dc)
        row = pos // half * band + pos % half * chip_rows
        return remote(send[kind].at[eight(target * CAP)], recv[kind].at[eight(row + c * CAP)],
                      zs.at[kind, 2 * pos + dc], zr.at[kind, 2 * pos + dc], (p, i, target))

    def own(kind):
        return pltpu.make_async_copy(send[kind].at[eight(e * CAP)], recv[kind].at[eight(c * CAP)], lsem.at[7 + kind])

    def x_copy(kind, pos, way):
        return remote(recv[kind].at[group(pos, 0)], recv[kind].at[group(pos, 2 - way)],
                      xs.at[kind, pos, way], xr.at[kind, pos, way], sides[way])

    def f_way(kind, pos):
        return (pos + kind) % 2

    def f_copy(kind, pos):
        way = f_way(kind, pos)
        return remote(recv[kind].at[group(pos, 2 - way)], recv[kind].at[group(pos, 3)],
                      fs.at[kind, pos], fr.at[kind, pos], sides[way])

    def z_send(kind, pos):
        for dc in (0, 1):
            if (pos, dc) == (0, 0):
                own(kind).start()
            else:
                z_copy(kind, pos, dc).start()

    def z_step(kind, pos):
        for dc in (0, 1):
            if (pos, dc) == (0, 0):
                own(kind).wait()
            else:
                z_copy(kind, pos, dc).wait_recv()
        for way in (0, 1):
            x_copy(kind, pos, way).start()

    def forward(kind, pos):
        x_copy(kind, pos, f_way(kind, pos)).wait_recv()
        f_copy(kind, pos).start()

    def direct_in(kind, h):
        for pos in range(h * half, (h + 1) * half):
            x_copy(kind, pos, 1 - f_way(kind, pos)).wait_recv()

    def opposite_in(kind, h):
        for pos in range(h * half, (h + 1) * half):
            f_copy(kind, pos).wait_recv()

    def map_copy():
        return remote(smap, next_hbm, ms.at[0], mr.at[0], (prev, i, e))

    def rows(h, slot, count):
        return slice(h * band + slot * share, h * band + (slot + count) * share)

    def inner(h, slot, count):
        r = rows(h, slot, count)
        gu[r, 0:hs] = jnp.dot(rx[r, :], wg[...], preferred_element_type=F32)
        gu[r, hs:] = jnp.dot(rx[r, :], wu[...], preferred_element_type=F32)

    def act(h, slot, count):
        r = rows(h, slot, count)
        n = count * share
        gate, up = gu[r, 0:hs], gu[r, hs:]
        gh = lax.dot_general(rg[r, :], wd[...], nt, preferred_element_type=F32)
        sig = jax.nn.sigmoid(gate)
        swish = gate * sig
        hidden = swish * up
        total = jnp.sum(hidden * gh, axis=1, keepdims=True)
        lane = lax.broadcasted_iota(jnp.int32, (n, 128), 1)
        row = jnp.bitwise_and(lax.broadcasted_iota(jnp.int32, (n, 128), 0), CAP - 1)
        spread = jnp.where(lane == row, jnp.broadcast_to(total, (n, 128)), 0.0)
        score[r.start // CAP:r.stop // CAP] = jnp.sum(spread.reshape(n // CAP, CAP, 128), axis=1, keepdims=True)
        hid[r, :] = hidden.astype(BF16)
        delta[r, 0:hs] = (gh * up * sig * (1.0 + gate * (1.0 - sig))).astype(BF16)
        delta[r, hs:] = (gh * swish).astype(BF16)

    def partial(h, slot, count):
        r = rows(h, slot, count)
        dg, du = delta[r, 0:hs], delta[r, hs:]
        wide = 512
        for t in range(width // wide):
            cut = slice(t * wide, (t + 1) * wide)
            value = lax.dot_general(dg, wg[cut, :], nt, preferred_element_type=F32)
            value += lax.dot_general(du, wu[cut, :], nt, preferred_element_type=F32)
            part[r, cut] = value.astype(BF16)

    def mine(h):
        return slice(h * share, (h + 1) * share)

    def cols(q):
        return slice(pieces[q][1], pieces[q][1] + pieces[q][2])

    def step1(q):
        h = pieces[q][0]
        return remote(part.at[rows(h, 3, 1), cols(q)], b1.at[mine(h), cols(q)], s1s.at[q], s1r.at[q], sides[q % 2])

    def plain(q):
        h = pieces[q][0]
        return remote(part.at[rows(h, 2 - q % 2, 1), cols(q)], bu.at[mine(h), cols(q)], sus.at[q], sur.at[q],
                      sides[1 - q % 2])

    def step2(q):
        h = pieces[q][0]
        return remote(b1.at[mine(h), cols(q)], b2.at[mine(h), cols(q)], s2s.at[q], s2r.at[q], sides[q % 2])

    def score_x(s, h):
        blocks = share // CAP
        n = (s - 1) * 2 + h
        return remote(score.at[pl.ds((h * nd + s) * blocks, blocks)], sc3.at[s - 1, pl.ds(h * blocks, blocks)],
                      cs.at[n], cr.at[n], peers[s])

    def score_z(pos, dc):
        target = mod(z + Z_PLACES[pos], nz) * 2 + core(dc)
        return remote(own_score.at[2 * pos + core(dc)], score_hbm.at[e], es.at[2 * pos + dc], er.at[2 * pos + dc],
                      (p, i, target))

    def score_own():
        return pltpu.make_async_copy(own_score.at[c], score_hbm.at[e], lsem.at[9])

    def y_copy(pair, pos, dc):
        h, start, size = pieces[2 * pair]
        wide = pl.ds(start, 2 * size)
        target = mod(z + Z_PLACES[pos], nz) * 2 + core(dc)
        n = pos % half * 2 + dc
        return remote(fin.at[eight(pos * chip_rows + core(dc) * CAP), wide], rows_hbm.at[eight(e * CAP), wide],
                      ys.at[pair, n], yr.at[pair, n], (prev, i, target))

    def all_y(pair):
        h = pieces[2 * pair][0]
        return [y_copy(pair, pos, dc) for pos in range(h * half, (h + 1) * half) for dc in (0, 1)]

    def both(copy, pair):
        for q in (2 * pair, 2 * pair + 1):
            copy(q).start()

    def middle(pair):
        for q in (2 * pair, 2 * pair + 1):
            h = pieces[q][0]
            step1(q).wait_recv()
            total = part[rows(h, 1 + q % 2, 1), cols(q)].astype(F32) + b1[mine(h), cols(q)].astype(F32)
            b1[mine(h), cols(q)] = total.astype(BF16)
            step2(q).start()

    def finish(pair):
        h = pieces[2 * pair][0]
        for q in (2 * pair, 2 * pair + 1):
            plain(q).wait_recv()
            step2(q).wait_recv()
            total = (part[rows(h, 0, 1), cols(q)].astype(F32) + b2[mine(h), cols(q)].astype(F32)
                     + bu[mine(h), cols(q)].astype(F32))
            fin[mine(h), cols(q)] = total.astype(BF16)
        for copy in all_y(pair):
            copy.start()

    first, second = len(PAIRS[0]), len(PAIRS[1])

    for pos in range(LOOK):
        z_send(0, pos)
    loads[3].wait()
    sg[...] = (slot_weight * jnp.dot(table, dyv[...], preferred_element_type=F32)).astype(BF16)
    for pos in range(LOOK):
        z_send(1, pos)
    pl.semaphore_signal(go, inc=1, device_id=(nxt, i, e), device_id_type=MESH)
    for copy in loads[4:]:
        copy.wait()
    steps = [(kind, pos) for pos in range(places) for kind in (0, 1)]
    for t, (kind, pos) in enumerate(steps):
        z_step(kind, pos)
        if kind == 1 and pos + LOOK < places:
            z_send(0, pos + LOOK)
            z_send(1, pos + LOOK)
        if t >= LAG:
            forward(*steps[t - LAG])
        if t == 11:
            direct_in(0, 0)
            opposite_in(0, 0)
            inner(0, 0, nd)
        if t == 12:
            direct_in(1, 0)
            opposite_in(1, 0)
            act(0, 0, nd)
        if t == 14:
            partial(0, 3, 1)
            for pair in range(first):
                both(step1, pair)
    forward(*steps[12])
    forward(*steps[13])
    partial(0, 1, 2)
    forward(*steps[14])
    forward(*steps[15])
    middle(0)
    both(plain, 0)
    for pair in range(1, first):
        middle(pair)
        both(plain, pair)
    pl.semaphore_wait(go, 1)
    map_copy().start()
    partial(0, 0, 1)
    direct_in(0, 1)
    inner(1, 0, nd - 1)
    opposite_in(0, 1)
    inner(1, 3, 1)
    direct_in(1, 1)
    act(1, 0, nd - 1)
    opposite_in(1, 1)
    act(1, 3, 1)
    partial(1, 3, 1)
    for pair in range(first, first + second):
        both(step1, pair)
    partial(1, 1, 2)
    both(plain, first)
    for s in range(1, nd):
        for h in (0, 1):
            score_x(s, h).start()
    saves = [pltpu.make_async_copy(a, b, lsem.at[10 + n]) for n, (a, b) in enumerate(
        ((rx, rx_hbm), (rg, rg_hbm), (delta, delta_hbm), (hid, hidden_hbm), (smap, smap_hbm)))]
    for copy in saves:
        copy.start()
    partial(1, 0, 1)
    for pair in range(first):
        finish(pair)
    for pair in range(first, first + second):
        middle(pair)
        if pair + 1 < first + second:
            both(plain, pair + 1)
    finish(first)
    for s in range(1, nd):
        for h in (0, 1):
            score_x(s, h).wait_recv()
    blocks = share // CAP
    for h in (0, 1):
        here = slice(h * blocks, (h + 1) * blocks)
        own_score[here] = (score[h * nd * blocks:h * nd * blocks + blocks]
                           + sc3[0, here] + sc3[1, here] + sc3[2, here])
    score_own().start()
    for pos in range(places):
        for dc in (0, 1):
            if (pos, dc) != (0, 0):
                score_z(pos, dc).start()
    for pair in range(first + 1, first + second):
        finish(pair)

    for copy in saves:
        copy.wait()
    for kind in (0, 1):
        for pos in range(places):
            for dc in (0, 1):
                if (pos, dc) != (0, 0):
                    z_copy(kind, pos, dc).wait_send()
            for way in (0, 1):
                x_copy(kind, pos, way).wait_send()
            f_copy(kind, pos).wait_send()
    for q in range(len(pieces)):
        step1(q).wait_send()
        plain(q).wait_send()
        step2(q).wait_send()
    map_copy().wait_send()
    map_copy().wait_recv()
    score_own().wait()
    for s in range(1, nd):
        for h in (0, 1):
            score_x(s, h).wait_send()
    for pos in range(places):
        for dc in (0, 1):
            if (pos, dc) != (0, 0):
                score_z(pos, dc).wait_send()
                score_z(pos, dc).wait_recv()
    for pair in range(len(pieces) // 2):
        for copy in all_y(pair):
            copy.wait_send()
            copy.wait_recv()


def routed(acts, grads, ids, weights, wg, wu, wd, nd, ne):
    tokens, width = acts.shape
    hs = wg.shape[1]
    slots = ne * CAP
    rows = nd * slots
    pieces = []
    for h, sizes in enumerate(PAIRS):
        start = 0
        for size in sizes:
            pieces += [(h, start, size // 2), (h, start + size // 2, size // 2)]
            start += size
    hbm = pl.BlockSpec(memory_space=pltpu.HBM)
    dma = pltpu.SemaphoreType.DMA
    places, n = len(Z_PLACES), len(pieces)
    shape = jax.ShapeDtypeStruct
    block = pltpu.VMEM((slots, width), BF16)
    full = pltpu.VMEM((rows, width), BF16)
    return pl.pallas_call(
        functools.partial(routed_kernel, nd, ne, pieces),
        out_shape=(shape((slots, width), BF16), shape((slots, tokens), BF16), shape((ne, 1, 128), F32),
                   shape((slots, tokens), BF16), shape((rows, width), BF16), shape((rows, width), BF16),
                   shape((rows, 2 * hs), BF16), shape((rows, hs), BF16)),
        in_specs=[hbm] * 7,
        out_specs=(hbm,) * 8,
        scratch_shapes=[pltpu.VMEM((tokens, width), BF16), pltpu.VMEM((tokens, width), BF16),
                        pltpu.VMEM(ids.shape, jnp.int32), pltpu.VMEM(ids.shape, F32), pltpu.VMEM((slots, tokens), BF16),
                        block, block, full, full, pltpu.VMEM(wg.shape, BF16), pltpu.VMEM(wu.shape, BF16),
                        pltpu.VMEM(wd.shape, BF16), pltpu.VMEM((rows, 2 * hs), F32), pltpu.VMEM((rows, 2 * hs), BF16),
                        pltpu.VMEM((rows, hs), BF16), full, block, block, block, block,
                        pltpu.VMEM((nd * ne, 1, 128), F32), pltpu.VMEM((nd - 1, ne, 1, 128), F32),
                        pltpu.VMEM((ne, 1, 128), F32),
                        dma((15,)), dma((2, ne)), dma((2, ne)), dma((2, places, 2)), dma((2, places, 2)),
                        dma((2, places)), dma((2, places))] + [dma((n,))] * 6 + [dma((n // 2, ne // 2))] * 2
        + [dma((2 * (nd - 1),))] * 2 + [dma((ne,))] * 2 + [dma((1,))] * 2 + [pltpu.SemaphoreType.REGULAR],
        compiler_params=pltpu.CompilerParams(collective_id=0, has_side_effects=True, vmem_limit_bytes=VMEM_LIMIT),
        name="routed",
    )(acts, grads, ids, weights, wg, wu, wd)


def local_kernel(rx, rg, delta, hid, rows, snext, smap, score, ids_ref, w_ref, out, gwg, dwg, dwu, dwd):
    tn = (((0,), (0,)), ((), ()))
    hs = hid.shape[1]
    slots, tokens = smap.shape

    @pl.when(pl.program_id(0) == 0)
    def _():
        ne = slots // CAP
        column = jnp.broadcast_to(score[...], (ne, CAP, 128)).reshape(slots, 128)
        expert, _ = slot_maps(ids_ref, slots, tokens)
        lane = lax.broadcasted_iota(jnp.int32, (slots, 128), 1)
        row = jnp.bitwise_and(lax.broadcasted_iota(jnp.int32, (slots, 128), 0), CAP - 1)
        column = jnp.sum(jnp.where(lane == row, column, 0.0), axis=1, keepdims=True)
        spread = smap[...].astype(F32) * column
        for k in range(ids_ref.shape[0]):
            picked = jnp.sum(jnp.where(ids_ref[k] == expert, spread, 0.0), axis=0, keepdims=True)
            gwg[k] = picked / w_ref[k]

    out[...] = lax.dot_general(snext[...], rows[...], tn, preferred_element_type=F32).astype(BF16)
    both = lax.dot_general(rx[...], delta[...], tn, preferred_element_type=F32).astype(BF16)
    dwg[...] = both[:, :hs]
    dwu[...] = both[:, hs:]
    dwd[...] = lax.dot_general(hid[...], rg[...], tn, preferred_element_type=F32).astype(BF16)


def local(rows, snext, score, smap, rx, rg, delta, hid, ids, weights):
    count, width = rx.shape
    hs = hid.shape[1]
    slots, tokens = smap.shape
    wide = 768

    def whole(array):
        return pl.BlockSpec(array.shape, lambda t: (0,) * array.ndim)

    def across(height):
        return pl.BlockSpec((height, wide), lambda t: (0, t))

    down = pl.BlockSpec((wide, hs), lambda t: (t, 0))
    shape = jax.ShapeDtypeStruct
    return pl.pallas_call(
        local_kernel,
        grid=(width // wide,),
        out_shape=(shape((tokens, width), BF16), shape(ids.shape, F32), shape((width, hs), BF16),
                   shape((width, hs), BF16), shape((hs, width), BF16)),
        in_specs=[across(count), across(count), whole(delta), whole(hid), across(slots), whole(snext), whole(smap),
                  whole(score), whole(ids), whole(weights)],
        out_specs=(across(tokens), whole(ids), down, down, across(hs)),
        compiler_params=pltpu.CompilerParams(vmem_limit_bytes=VMEM_LIMIT),
        name="local",
    )(rx, rg, delta, hid, rows, snext, smap, score, ids, weights)


def shards(block_input, output_grad, expert_ids, gate_weights, gate_proj, up_proj, down_proj):
    nd, ne = lax.axis_size("dp"), lax.axis_size("expert")
    ids = jnp.transpose(expert_ids, (2, 0, 1))
    weights = jnp.transpose(gate_weights, (2, 0, 1))
    outs = routed(block_input[0], output_grad[0], ids, weights, gate_proj[0, 0], up_proj[0, 0], down_proj[0, 0],
                  nd, ne)
    received, gwg, dwg, dwu, dwd = local(*outs, ids, weights)
    return (received[None], jnp.transpose(gwg, (1, 2, 0)), dwg[None, None], dwu[None, None], dwd[None, None])


def solution(mesh):
    in_specs = (
        P("pipe", ("dp", "expert"), None),
        P("pipe", ("dp", "expert"), None),
        P("pipe", ("dp", "expert"), None),
        P("pipe", ("dp", "expert"), None),
        P("pipe", "expert", None, "dp"),
        P("pipe", "expert", None, "dp"),
        P("pipe", "expert", "dp", None),
    )
    out_specs = (
        P("pipe", ("dp", "expert"), None),
        P("pipe", ("dp", "expert"), None),
        P("pipe", "expert", None, "dp"),
        P("pipe", "expert", None, "dp"),
        P("pipe", "expert", "dp", None),
    )
    return jax.shard_map(shards, mesh=mesh, in_specs=in_specs, out_specs=out_specs, check_vma=False)
```
